32 devices in a mesh: dp: 8 (over z, y), tensor: 4 (over x, core).
Axes of the slice: x: 2, y: 2, z: 4, core: 2. Of those that a mesh axis runs over, the one named last changes fastest.
Arguments:
- tokens: bfloat16 [32, 1024, 768], P(('dp', 'tensor')), may hold values from -6 to 6
- segments: int32 [32, 1024], P(('dp', 'tensor')), may hold values from 0 to 18, as said below
- projections: bfloat16 [3, 768, 768], P(None, None, 'tensor'), may hold values from -0.21875 to 0.21875
- query_value_bias: bfloat16 [2, 768], P(None, 'tensor'), may hold values from -3 to 3
- out_weight: bfloat16 [768, 768], P('tensor'), may hold values from -0.875 to 0.875
- out_bias: float32 [768], replicated, may hold values from -3 to 3
- first_gain: float32 [768], replicated, may hold values from 0.5 to 1.5
- first_shift: float32 [768], replicated, may hold values from -2 to 2
- up_weight: bfloat16 [768, 3072], P(None, 'tensor'), may hold values from -0.21875 to 0.21875
- up_bias: bfloat16 [3072], P('tensor'), may hold values from -3 to 3
- down_weight: bfloat16 [3072, 768], P('tensor'), may hold values from -0.109375 to 0.109375
- down_bias: float32 [768], replicated, may hold values from -2 to 2
- second_gain: float32 [768], replicated, may hold values from 0.5 to 1.5
- second_shift: float32 [768], replicated, may hold values from -2 to 2
- cotangent: bfloat16 [32, 1024, 768], P(('dp', 'tensor')), may hold values from -6 to 6
Outputs:
- output: bfloat16 [32, 1024, 768], P(('dp', 'tensor'))
- grad_tokens: bfloat16 [32, 1024, 768], P(('dp', 'tensor'))
- grad_projections: float32 [3, 768, 768], P(None, None, 'tensor')
- grad_query_value_bias: float32 [2, 768], P(None, 'tensor')
- grad_out_weight: float32 [768, 768], P('tensor')
- grad_out_bias: float32 [768], replicated
- grad_first_gain: float32 [768], replicated
- grad_first_shift: float32 [768], replicated
- grad_up_weight: float32 [768, 3072], P(None, 'tensor')
- grad_up_bias: float32 [3072], P('tensor')
- grad_down_weight: float32 [3072, 768], P('tensor')
- grad_down_bias: float32 [768], replicated
- grad_second_gain: float32 [768], replicated
- grad_second_shift: float32 [768], replicated
- root_means: float32 [3], replicated
The draws below stay inside these ranges and needn't reach their ends.
Inputs may be any that keep to these rules, and one draw needn't show every extreme that they name: Within each sequence the nonzero numbers are 1, 2, 3, ... in order along the positions, each held by one run of consecutive positions of max(60, 2) to 800 positions, except that the last run before the padding may be shorter; 0 marks padding, a suffix of fewer than 128 positions that may be empty. The first sequence has no padding and all its runs but the last have the shortest length, so it holds the most segments.
All inputs are finite; a program needn't handle non-finite values.
Results may differ from the reference program's by a relative error of at most 0.02.
Values may be sent and summed in bfloat16 or wider, within the bound.
No kernel may reach another device: no remote copies, remote signals or barrier semaphores. Data moves between devices by JAX's collectives and lax.ppermute only.
A program may use at most 192 MiB of HBM per device.

```python
from functools import partial
import jax
import jax.numpy as jnp
from jax import lax

D = 768
HEADS = 12
HEAD = 64
FF = 3072
L = 1024
SEQS = 32


def draw_segments(key, part):
    shortest = max(L * 60 // 1024, 2)
    longest = max(L * 800 // 1024 + 1, shortest + 1)
    number = L // shortest + 1
    length_key, pad_key = jax.random.split(key)
    first_row = (jnp.arange(SEQS, dtype=jnp.int32) == 0)[:, None]
    lengths = jax.random.randint(length_key, (SEQS, number), shortest, longest, dtype=jnp.int32)
    lengths = jnp.where(first_row, shortest, lengths)
    ends = jnp.cumsum(lengths, axis=1)
    pads = jax.random.randint(pad_key, (SEQS, 1), 0, max(L // 8, 1), dtype=jnp.int32)
    pads = jnp.where(first_row, 0, pads)
    places = jnp.arange(L, dtype=jnp.int32)[None, :]
    numbers = 1 + jnp.sum((places[:, :, None] >= ends[:, None, :]).astype(jnp.int32), axis=2)
    return jnp.where(places < L - pads, numbers, 0).astype(jnp.int32)


def block_levels(key, shape, shards, low, high):
    level = 1.0
    for position, shards_of in shards:
        steps = jax.random.uniform(jax.random.fold_in(jax.random.fold_in(key, 6), position), (shards_of,), jnp.float32, low / len(shards), high / len(shards))
        level = level * jnp.repeat(jnp.exp(steps), shape[position] // shards_of).reshape((-1,) + (1,) * (len(shape) - 1 - position))
    return level


def scatter_about(stream_key, dims, deviation, limit, pieces=(), kind=jnp.bfloat16):
    values = jax.random.normal(stream_key, dims, jnp.float32) * deviation
    if len(pieces) > 0:
        values = block_levels(stream_key, dims, pieces, -0.22, 0.18) * values
    return jnp.clip(values, min=-limit, max=limit).astype(kind)


def setup_inputs(seed: int = 0) -> dict:
    seeds = jax.random.split(jax.random.key(seed), 16)
    tokens = scatter_about(seeds[0], (SEQS, L, D), 1.0, 6.0, ((0, 32),))
    segments = draw_segments(jax.random.fold_in(seeds[15], 71), 0)
    projections = scatter_about(seeds[2], (3, D, D), D ** -0.5, 0.21875, ((2, 4),))
    query_value_bias = scatter_about(seeds[3], (2, D), 0.5, 3.0, ((1, 4),))
    out_weight = scatter_about(seeds[4], (D, D), (D // 16) ** -0.5, 0.875, ((0, 4),))
    out_bias = scatter_about(seeds[5], (D,), 0.5, 3.0, (), jnp.float32)
    first_gain = jnp.clip(1.0 + 0.1 * jax.random.normal(seeds[6], (D,), jnp.float32), 0.5, 1.5)
    first_shift = scatter_about(seeds[7], (D,), 0.3, 2.0, (), jnp.float32)
    up_weight = scatter_about(seeds[8], (D, FF), D ** -0.5, 0.21875, ((1, 4),))
    up_bias = scatter_about(seeds[9], (FF,), 0.5, 3.0, ((0, 4),))
    down_weight = scatter_about(seeds[10], (FF, D), FF ** -0.5, 0.109375, ((0, 4),))
    down_bias = scatter_about(seeds[11], (D,), 0.3, 2.0, (), jnp.float32)
    second_gain = jnp.clip(1.0 + 0.1 * jax.random.normal(seeds[12], (D,), jnp.float32), 0.5, 1.5)
    second_shift = scatter_about(seeds[13], (D,), 0.3, 2.0, (), jnp.float32)
    cotangent = scatter_about(seeds[14], (SEQS, L, D), 1.0, 6.0, ((0, 32),))
    return {"tokens": tokens, "segments": segments, "projections": projections, "query_value_bias": query_value_bias, "out_weight": out_weight, "out_bias": out_bias, "first_gain": first_gain, "first_shift": first_shift, "up_weight": up_weight, "up_bias": up_bias, "down_weight": down_weight, "down_bias": down_bias, "second_gain": second_gain, "second_shift": second_shift, "cotangent": cotangent}


@jax.custom_vjp
def low(v):
    return lax.optimization_barrier(v.astype(jnp.bfloat16)).astype(jnp.float32)

@jax.custom_vjp
def low_back(v):
    return v

def low_keep(v):
    return (low(v), None)

def low_pass(kept, grad):
    return (grad,)

def back_keep(v):
    return (v, None)

def back_low(kept, grad):
    return (low(grad),)
low.defvjp(low_keep, low_pass)
low_back.defvjp(back_keep, back_low)
highest = lax.Precision.HIGHEST
epsilon = 1e-06

def normalize(values, gain, shift):
    mean = lax.optimization_barrier(jnp.mean(values, axis=-1, keepdims=True))
    centred = values - mean
    variance = lax.optimization_barrier(jnp.mean(centred * centred, axis=-1, keepdims=True))
    return centred * lax.rsqrt(variance + epsilon) * gain + shift

def gelu(values):
    return 0.5 * values * (1.0 + lax.erf(values * 0.7071067811865476))

def forward(params, tokens, labels):
    projections, query_value_bias, out_weight, out_bias, first_gain, first_shift, up_weight, up_bias, down_weight, down_bias, second_gain, second_shift = params
    projected = jnp.einsum('td,pde->pte', tokens, projections, precision=highest)
    queries = low(low_back(projected[0] + query_value_bias[0]))
    keys = low(low_back(projected[1]))
    values = low(low_back(projected[2] + query_value_bias[1]))
    split_shape = (L, HEADS, HEAD)
    scores = jnp.einsum('qhd,khd->hqk', queries.reshape(split_shape), keys.reshape(split_shape), precision=highest) * HEAD ** (-0.5)
    scores = low_back(scores)
    same = labels[:, None] == labels[None, :]
    scores = jnp.where(same[None], scores, -1e+30)
    maximum = lax.optimization_barrier(jnp.max(scores, axis=2, keepdims=True))
    exponents = jnp.exp(scores - maximum)
    weights = low(exponents / lax.optimization_barrier(jnp.sum(exponents, axis=2, keepdims=True)))
    context = jnp.einsum('hqk,khd->qhd', weights, values.reshape(split_shape), precision=highest).reshape(L, D)
    context = low_back(low(context))
    attention = low_back(jnp.dot(context, out_weight, precision=highest)) + out_bias
    hidden = normalize(tokens + attention, first_gain, first_shift)
    up = low_back(jnp.dot(low(hidden), up_weight, precision=highest) + up_bias)
    active = low(gelu(up))
    feed = low_back(jnp.dot(active, down_weight, precision=highest)) + down_bias
    output = normalize(hidden + feed, second_gain, second_shift)
    return (output, attention, feed)

def reference(tokens, segments, projections, query_value_bias, out_weight, out_bias, first_gain, first_shift, up_weight, up_bias, down_weight, down_bias, second_gain, second_shift, cotangent):
    params = tuple((item.astype(jnp.float32) for item in (projections, query_value_bias, out_weight, out_bias, first_gain, first_shift, up_weight, up_bias, down_weight, down_bias, second_gain, second_shift)))

    def step(totals, block):
        rows, labels, grad_rows = block
        valid = (labels != 0).astype(jnp.float32)[:, None]
        (output, attention, feed), pullback = jax.vjp(partial(forward, labels=labels), params, rows.astype(jnp.float32))
        weight_grads, input_grad = pullback((grad_rows.astype(jnp.float32) * valid, jnp.zeros_like(attention), jnp.zeros_like(feed)))
        stats = jnp.stack([jnp.sum(output * output * valid), jnp.sum(attention * attention * valid), jnp.sum(feed * feed * valid), jnp.sum(valid)])
        totals = jax.tree.map(lambda left, right: left + right, totals, (weight_grads, stats))
        return (totals, (output.astype(jnp.bfloat16), input_grad.astype(jnp.bfloat16)))
    start = (jax.tree.map(jnp.zeros_like, params), jnp.zeros((4,), jnp.float32))
    (weight_grads, stats), (outputs, input_grads) = lax.scan(step, start, (tokens, segments, cotangent))
    root_means = jnp.sqrt(stats[:3] / (stats[3] * D))
    return (outputs, input_grads, weight_grads[0], weight_grads[1], weight_grads[2], weight_grads[3], weight_grads[4], weight_grads[5], weight_grads[6], weight_grads[7], weight_grads[8], weight_grads[9], weight_grads[10], weight_grads[11], root_means)
```

```python
import jax
import jax.numpy as jnp
from jax import lax
from jax.experimental import pallas as pl
from jax.experimental.pallas import tpu as pltpu
from jax.sharding import PartitionSpec as P

HEAD = 64
EPSILON = 1e-06
BLOCK = 256
F32 = jnp.float32
BF16 = jnp.bfloat16


NT = (((1,), (1,)), ((), ()))
NN = (((1,), (0,)), ((), ()))
TN = (((0,), (0,)), ((), ()))


def mm(left, right, dims=NN):
    return lax.dot_general(left, right, dims, preferred_element_type=F32)


def bits_of(size):
    return [1 << b for b in range(size.bit_length() - 1)]


def swap(value, axis, bit):
    size = lax.axis_size(axis)
    return lax.ppermute(value, axis, [(i, i ^ bit) for i in range(size)])


def gather_shards(own, size):
    pieces = {0: own}
    for bit in reversed(bits_of(size)):
        for r in list(pieces):
            pieces[r | bit] = swap(pieces[r], "tensor", bit)
    return pieces


def add_low(left, right):
    return (left.astype(F32) + right.astype(F32)).astype(left.dtype)


def reduce_shards(pieces, size):
    for bit in bits_of(size):
        pieces = {
            r: add_low(pieces[r], swap(pieces[r | bit], "tensor", bit))
            for r in pieces
            if not r & bit
        }
    return pieces[0]


def reduce_copies(value):
    size = lax.axis_size("dp")
    me = lax.axis_index("dp")
    for bit in bits_of(size):
        high = (me & bit) != 0
        half = value.shape[0] // 2
        low_part, high_part = value[:half], value[half:]
        sent = jnp.where(high, low_part, high_part)
        kept = jnp.where(high, high_part, low_part)
        value = add_low(kept, swap(sent, "dp", bit))
    for bit in reversed(bits_of(size)):
        high = (me & bit) != 0
        other = swap(value, "dp", bit)
        value = jnp.concatenate(
            [jnp.where(high, other, value), jnp.where(high, value, other)], axis=0
        )
    return value


def total_small(value, axes):
    for axis in axes:
        for bit in bits_of(lax.axis_size(axis)):
            value = value + swap(value, axis, bit)
    return value


def attend_kernel(qkv_ref, all_ref, column_ref, row_ref, context_ref, logsum_ref, bias_ref):
    share = context_ref.shape[1]
    heads = share // HEAD
    scale = HEAD ** (-0.5)
    bias_ref[...] = jnp.where(column_ref[:, :1] == row_ref[...], 0.0, -1e30)
    for h in range(heads):
        at = h * HEAD
        queries = qkv_ref[:, at : at + HEAD] * jnp.asarray(scale, BF16)
        keys = all_ref[:, share + at : share + at + HEAD]
        values = all_ref[:, 2 * share + at : 2 * share + at + HEAD]
        scores = mm(keys, queries, NT) + bias_ref[...]
        maximum = jnp.max(scores, axis=0, keepdims=True)
        exponents = jnp.exp(scores - maximum)
        total = jnp.sum(exponents, axis=0, keepdims=True)
        context = mm(values.T, exponents.astype(BF16)) / total
        context_ref[:, at : at + HEAD] = context.T.astype(BF16)
        logsum_ref[h : h + 1, :] = maximum + jnp.log(total)


def attend(qkv, column, row):
    length, width = qkv.shape
    share = width // 3
    heads = share // HEAD
    block = min(BLOCK, length)
    steps = length // block
    return pl.pallas_call(
        attend_kernel,
        grid=(steps,),
        in_specs=[
            pl.BlockSpec((block, width), lambda i: (i, 0)),
            pl.BlockSpec((length, width), lambda i: (0, 0)),
            pl.BlockSpec((length, 128), lambda i: (0, 0)),
            pl.BlockSpec((1, block), lambda i: (0, i)),
        ],
        out_specs=[
            pl.BlockSpec((block, share), lambda i: (i, 0)),
            pl.BlockSpec((heads, block), lambda i: (0, i)),
        ],
        out_shape=[
            jax.ShapeDtypeStruct((length, share), BF16),
            jax.ShapeDtypeStruct((heads, length), F32),
        ],
        scratch_shapes=[pltpu.VMEM((length, block), F32)],
        cost_estimate=pl.CostEstimate(
            flops=16 * heads * length * length * HEAD,
            transcendentals=heads * length * length,
            bytes_accessed=4 * length * width,
        ),
        name="attend",
    )(qkv, qkv, column, row)


def back_kernel(
    qkv_ref, all_ref, column_ref, row_ref, logsum_ref, grad_ref, query_ref, key_ref, value_ref,
    bias_ref, key_sum, value_sum,
):
    share = grad_ref.shape[1]
    heads = share // HEAD
    scale = HEAD ** (-0.5)
    step = pl.program_id(0)
    bias_ref[...] = jnp.where(column_ref[:, :1] == row_ref[...], 0.0, -1e30)

    @pl.when(step == 0)
    def _():
        key_sum[...] = jnp.zeros_like(key_sum)
        value_sum[...] = jnp.zeros_like(value_sum)

    for h in range(heads):
        at = h * HEAD
        queries = qkv_ref[:, at : at + HEAD] * jnp.asarray(scale, BF16)
        keys = all_ref[:, share + at : share + at + HEAD]
        values = all_ref[:, 2 * share + at : 2 * share + at + HEAD]
        grad = grad_ref[:, at : at + HEAD]
        scores = mm(keys, queries, NT) + bias_ref[...]
        weights = jnp.exp(scores - logsum_ref[h : h + 1, :])
        grad_weights = mm(values, grad, NT)
        correction = jnp.sum(grad_weights * weights, axis=0, keepdims=True)
        grad_scores = (weights * (grad_weights - correction)).astype(BF16)
        value_sum[h] += mm(weights.astype(BF16), grad)
        key_sum[h] += mm(grad_scores, queries)
        grad_queries = mm(keys.T, grad_scores) * scale
        query_ref[:, at : at + HEAD] = grad_queries.T.astype(BF16)

    @pl.when(step == pl.num_programs(0) - 1)
    def _():
        for h in range(heads):
            at = h * HEAD
            key_ref[:, at : at + HEAD] = key_sum[h].astype(BF16)
            value_ref[:, at : at + HEAD] = value_sum[h].astype(BF16)


def attend_back(qkv, column, row, logsum, grad):
    length, width = qkv.shape
    share = width // 3
    heads = share // HEAD
    block = min(BLOCK, length)
    steps = length // block
    parts = pl.pallas_call(
        back_kernel,
        grid=(steps,),
        in_specs=[
            pl.BlockSpec((block, width), lambda i: (i, 0)),
            pl.BlockSpec((length, width), lambda i: (0, 0)),
            pl.BlockSpec((length, 128), lambda i: (0, 0)),
            pl.BlockSpec((1, block), lambda i: (0, i)),
            pl.BlockSpec((heads, block), lambda i: (0, i)),
            pl.BlockSpec((block, share), lambda i: (i, 0)),
        ],
        out_specs=[
            pl.BlockSpec((block, share), lambda i: (i, 0)),
            pl.BlockSpec((length, share), lambda i: (0, 0)),
            pl.BlockSpec((length, share), lambda i: (0, 0)),
        ],
        out_shape=[jax.ShapeDtypeStruct((length, share), BF16)] * 3,
        scratch_shapes=[
            pltpu.VMEM((length, block), F32),
            pltpu.VMEM((heads, length, HEAD), F32),
            pltpu.VMEM((heads, length, HEAD), F32),
        ],
        cost_estimate=pl.CostEstimate(
            flops=40 * heads * length * length * HEAD,
            transcendentals=heads * length * length,
            bytes_accessed=8 * length * width,
        ),
        name="attend_back",
    )(qkv, qkv, column, row, logsum, grad)
    return jnp.concatenate(parts, axis=1)


def center(values):
    mean = jnp.mean(values, axis=-1, keepdims=True)
    centred = values - mean
    variance = jnp.mean(centred * centred, axis=-1, keepdims=True)
    rate = lax.rsqrt(variance + EPSILON)
    return centred * rate, rate


def center_back(grad, normal, rate):
    return (
        grad
        - jnp.mean(grad, axis=-1, keepdims=True)
        - normal * jnp.mean(grad * normal, axis=-1, keepdims=True)
    ) * rate


def shards(
    tokens, segments, projections, query_value_bias, out_weight, out_bias, first_gain,
    first_shift, up_weight, up_bias, down_weight, down_bias, second_gain, second_shift, cotangent,
):
    size = lax.axis_size("tensor")
    local_seqs, length, width = tokens.shape
    share = projections.shape[2]
    hidden_share = up_weight.shape[1]
    order = range(size)
    rows = tokens.reshape(-1, width)
    wide = rows.astype(F32)
    valid = (segments != 0).astype(F32).reshape(-1, 1)
    label_rows = [segments[s : s + 1] for s in range(local_seqs)]
    label_columns = [
        jnp.broadcast_to(segments[s][:, None], (length, 128)) for s in range(local_seqs)
    ]

    proj_own = projections.transpose(0, 2, 1).reshape(3 * share, width)
    biases = jnp.concatenate([query_value_bias.reshape(-1), up_bias]).reshape(1, -1)
    biases = gather_shards(biases, size)
    proj = gather_shards(proj_own, size)
    outs = gather_shards(out_weight, size)
    ups = gather_shards(up_weight, size)
    downs = gather_shards(down_weight, size)

    def pieces(value):
        return [value[s * length : (s + 1) * length] for s in range(local_seqs)]

    def join(values):
        return values[0] if len(values) == 1 else jnp.concatenate(values, axis=0)

    qkv, logsums, contexts = {}, {}, {}
    for r in order:
        flat = biases[r][0]
        bias = jnp.concatenate([flat[:share], jnp.zeros((share,), BF16), flat[share : 2 * share]])
        qkv[r] = (mm(rows, proj[r], NT) + bias.astype(F32)).astype(BF16)
        got = [
            attend(part, label_columns[s], label_rows[s]) for s, part in enumerate(pieces(qkv[r]))
        ]
        contexts[r] = join([g[0] for g in got])
        logsums[r] = [g[1] for g in got]
    context = jnp.concatenate([contexts[r] for r in order], axis=1)
    out_all = jnp.concatenate([outs[r] for r in order], axis=0)
    attention = mm(context, out_all) + out_bias
    normal_one, rate_one = center(wide + attention)
    hidden = normal_one * first_gain + first_shift
    hidden_low = hidden.astype(BF16)
    active, slope = {}, {}
    feed = down_bias
    for r in order:
        up = mm(hidden_low, ups[r]) + biases[r][0, 2 * share :].astype(F32)
        phi = 0.5 * (1.0 + lax.erf(up * 0.7071067811865476))
        active[r] = (up * phi).astype(BF16)
        slope[r] = (phi + up * jnp.exp(-0.5 * up * up) * 0.3989422804014327).astype(BF16)
        feed = feed + mm(active[r], downs[r])
    normal_two, rate_two = center(hidden + feed)
    output = normal_two * second_gain + second_shift
    grad_output = cotangent.reshape(-1, width).astype(F32) * valid
    grad_two = center_back(grad_output * second_gain, normal_two, rate_two)
    grad_two_low = grad_two.astype(BF16)
    grad_down, grad_up, up_sums = {}, {}, {}
    grad_hidden = grad_two
    for r in reversed(order):
        grad_down[r] = mm(active[r], grad_two_low, TN).astype(BF16)
        up_grad = (mm(grad_two_low, downs[r], NT) * slope[r].astype(F32)).astype(BF16)
        grad_up[r] = mm(hidden_low, up_grad, TN).astype(BF16)
        up_sums[r] = jnp.sum(up_grad.astype(F32), axis=0, keepdims=True)
        grad_hidden = grad_hidden + mm(up_grad, ups[r], NT)
    total_down = reduce_copies(reduce_shards(grad_down, size))
    total_up = reduce_copies(reduce_shards(grad_up, size))
    total_up_bias = total_small(reduce_shards(up_sums, size), ("dp",))
    grad_one = center_back(grad_hidden * first_gain, normal_one, rate_one)
    grad_one_low = grad_one.astype(BF16)
    small = jnp.stack(
        [
            jnp.sum(grad_one, axis=0),
            jnp.sum(grad_hidden * normal_one, axis=0),
            jnp.sum(grad_hidden, axis=0),
            jnp.sum(grad_two, axis=0),
            jnp.sum(grad_output * normal_two, axis=0),
            jnp.sum(grad_output, axis=0),
            jnp.sum(output * output * valid, axis=0),
            jnp.sum(attention * attention * valid, axis=0),
            jnp.sum(feed * feed * valid, axis=0),
            jnp.broadcast_to(jnp.sum(valid) / width, (width,)),
        ]
    )
    small = total_small(small, ("tensor", "dp"))
    stats = jnp.sum(small[6:], axis=1)
    root_means = jnp.sqrt(stats[:3] / (stats[3] * width))
    grad_out_all = mm(context, grad_one_low, TN).astype(BF16)
    grad_out = {r: grad_out_all[r * share : (r + 1) * share] for r in order}
    total_out = reduce_copies(reduce_shards(grad_out, size))
    grad_proj, grad_bias = {}, {}
    grad_input = grad_one
    for r in reversed(order):
        grad_context = mm(grad_one_low, outs[r], NT).astype(BF16)
        stacked = join(
            [
                attend_back(part, label_columns[s], label_rows[s], logsums[r][s], grad)
                for s, (part, grad) in enumerate(zip(pieces(qkv[r]), pieces(grad_context)))
            ]
        )
        grad_proj[r] = mm(stacked, rows, TN).astype(BF16)
        sums = jnp.sum(stacked.astype(F32), axis=0)
        grad_bias[r] = jnp.stack([sums[:share], sums[2 * share :]])
        grad_input = grad_input + mm(stacked, proj[r])
    total_proj = reduce_copies(reduce_shards(grad_proj, size))
    total_bias = total_small(reduce_shards(grad_bias, size), ("dp",))
    total_proj = total_proj.astype(F32).reshape(3, share, width).transpose(0, 2, 1)
    return (
        output.astype(BF16).reshape(tokens.shape),
        grad_input.astype(BF16).reshape(tokens.shape),
        total_proj,
        total_bias,
        total_out.astype(F32),
        small[0],
        small[1],
        small[2],
        total_up.astype(F32),
        total_up_bias.reshape(hidden_share),
        total_down.astype(F32),
        small[3],
        small[4],
        small[5],
        root_means,
    )


def solution(mesh):
    both = P(("dp", "tensor"), None, None)
    column = P(None, "tensor")
    in_specs = (
        both, P(("dp", "tensor"), None), P(None, None, "tensor"), column, P("tensor", None),
        P(), P(), P(), column, P("tensor"), P("tensor", None), P(), P(), P(), both,
    )
    out_specs = (
        both, both, P(None, None, "tensor"), column, P("tensor", None), P(), P(), P(),
        column, P("tensor"), P("tensor", None), P(), P(), P(), P(),
    )
    return jax.shard_map(shards, mesh=mesh, in_specs=in_specs, out_specs=out_specs, check_vma=False)
```

```python
import jax
import jax.numpy as jnp
from jax import lax
from jax.experimental import pallas as pl
from jax.experimental.pallas import tpu as pltpu
from jax.sharding import PartitionSpec as P

HEAD = 64
EPSILON = 1e-06
BLOCK = 256
F32 = jnp.float32
BF16 = jnp.bfloat16


NT = (((1,), (1,)), ((), ()))
NN = (((1,), (0,)), ((), ()))
TN = (((0,), (0,)), ((), ()))


def mm(left, right, dims=NN):
    return lax.dot_general(left, right, dims, preferred_element_type=F32)


def bits_of(size):
    return [1 << b for b in range(size.bit_length() - 1)]


def swap(value, axis, bit):
    size = lax.axis_size(axis)
    return lax.ppermute(value, axis, [(i, i ^ bit) for i in range(size)])


def gather_shards(own, size):
    pieces = {0: own}
    for bit in reversed(bits_of(size)):
        for r in list(pieces):
            pieces[r | bit] = swap(pieces[r], "tensor", bit)
    return pieces


def add_low(left, right):
    return (left.astype(F32) + right.astype(F32)).astype(left.dtype)


def hold(*values):
    return lax.optimization_barrier(values)


class Copies:
    def __init__(self, value, bits):
        self.value = value
        self.todo = [(True, bit) for bit in bits] + [(False, bit) for bit in reversed(bits)]

    def step(self):
        if not self.todo:
            return
        down, bit = self.todo.pop(0)
        high = (lax.axis_index("dp") & bit) != 0
        value = self.value
        if down:
            half = value.shape[0] // 2
            low_part, high_part = value[:half], value[half:]
            sent = jnp.where(high, low_part, high_part)
            kept = jnp.where(high, high_part, low_part)
            self.value = add_low(kept, swap(sent, "dp", bit))
        else:
            other = swap(value, "dp", bit)
            self.value = jnp.concatenate(
                [jnp.where(high, other, value), jnp.where(high, value, other)], axis=0
            )

    def finish(self):
        while self.todo:
            self.step()
        return self.value


class Total:
    def __init__(self, value, axes):
        self.value = value
        self.todo = [(axis, bit) for axis in axes for bit in bits_of(lax.axis_size(axis))]

    def step(self):
        if self.todo:
            axis, bit = self.todo.pop(0)
            self.value = self.value + swap(self.value, axis, bit)

    def finish(self):
        while self.todo:
            self.step()
        return self.value


def place(pieces, size):
    me = lax.axis_index("tensor")
    rows = [pieces[r] for r in range(size)]
    return jnp.concatenate(
        [sum(jnp.where(me ^ r == t, rows[r], 0.0) for r in range(size)) for t in range(size)],
        axis=0,
    )


def attend_kernel(qkv_ref, all_ref, column_ref, row_ref, context_ref, logsum_ref, bias_ref):
    share = context_ref.shape[1]
    heads = share // HEAD
    scale = HEAD ** (-0.5)
    bias_ref[...] = jnp.where(column_ref[:, :1] == row_ref[...], 0.0, -1e30)
    for h in range(heads):
        at = h * HEAD
        queries = qkv_ref[:, at : at + HEAD] * jnp.asarray(scale, BF16)
        keys = all_ref[:, share + at : share + at + HEAD]
        values = all_ref[:, 2 * share + at : 2 * share + at + HEAD]
        scores = mm(keys, queries, NT) + bias_ref[...]
        maximum = jnp.max(scores, axis=0, keepdims=True)
        exponents = jnp.exp(scores - maximum)
        total = jnp.sum(exponents, axis=0, keepdims=True)
        context = mm(values.T, exponents.astype(BF16)) / total
        context_ref[:, at : at + HEAD] = context.T.astype(BF16)
        logsum_ref[h : h + 1, :] = maximum + jnp.log(total)


def attend(qkv, column, row):
    length, width = qkv.shape
    share = width // 3
    heads = share // HEAD
    block = min(BLOCK, length)
    steps = length // block
    return pl.pallas_call(
        attend_kernel,
        grid=(steps,),
        in_specs=[
            pl.BlockSpec((block, width), lambda i: (i, 0)),
            pl.BlockSpec((length, width), lambda i: (0, 0)),
            pl.BlockSpec((length, 128), lambda i: (0, 0)),
            pl.BlockSpec((1, block), lambda i: (0, i)),
        ],
        out_specs=[
            pl.BlockSpec((block, share), lambda i: (i, 0)),
            pl.BlockSpec((heads, block), lambda i: (0, i)),
        ],
        out_shape=[
            jax.ShapeDtypeStruct((length, share), BF16),
            jax.ShapeDtypeStruct((heads, length), F32),
        ],
        scratch_shapes=[pltpu.VMEM((length, block), F32)],
        cost_estimate=pl.CostEstimate(
            flops=16 * heads * length * length * HEAD,
            transcendentals=heads * length * length,
            bytes_accessed=4 * length * width,
        ),
        name="attend",
    )(qkv, qkv, column, row)


def back_kernel(
    qkv_ref, all_ref, column_ref, row_ref, logsum_ref, grad_ref, query_ref, key_ref, value_ref,
    bias_ref, key_sum, value_sum,
):
    share = grad_ref.shape[1]
    heads = share // HEAD
    scale = HEAD ** (-0.5)
    step = pl.program_id(0)
    bias_ref[...] = jnp.where(column_ref[:, :1] == row_ref[...], 0.0, -1e30)

    @pl.when(step == 0)
    def _():
        key_sum[...] = jnp.zeros_like(key_sum)
        value_sum[...] = jnp.zeros_like(value_sum)

    for h in range(heads):
        at = h * HEAD
        queries = qkv_ref[:, at : at + HEAD] * jnp.asarray(scale, BF16)
        keys = all_ref[:, share + at : share + at + HEAD]
        values = all_ref[:, 2 * share + at : 2 * share + at + HEAD]
        grad = grad_ref[:, at : at + HEAD]
        scores = mm(keys, queries, NT) + bias_ref[...]
        weights = jnp.exp(scores - logsum_ref[h : h + 1, :])
        grad_weights = mm(values, grad, NT)
        correction = jnp.sum(grad_weights * weights, axis=0, keepdims=True)
        grad_scores = (weights * (grad_weights - correction)).astype(BF16)
        value_sum[h] += mm(weights.astype(BF16), grad)
        key_sum[h] += mm(grad_scores, queries)
        grad_queries = mm(keys.T, grad_scores) * scale
        query_ref[:, at : at + HEAD] = grad_queries.T.astype(BF16)

    @pl.when(step == pl.num_programs(0) - 1)
    def _():
        for h in range(heads):
            at = h * HEAD
            key_ref[:, at : at + HEAD] = key_sum[h].astype(BF16)
            value_ref[:, at : at + HEAD] = value_sum[h].astype(BF16)


def attend_back(qkv, column, row, logsum, grad):
    length, width = qkv.shape
    share = width // 3
    heads = share // HEAD
    block = min(BLOCK, length)
    steps = length // block
    parts = pl.pallas_call(
        back_kernel,
        grid=(steps,),
        in_specs=[
            pl.BlockSpec((block, width), lambda i: (i, 0)),
            pl.BlockSpec((length, width), lambda i: (0, 0)),
            pl.BlockSpec((length, 128), lambda i: (0, 0)),
            pl.BlockSpec((1, block), lambda i: (0, i)),
            pl.BlockSpec((heads, block), lambda i: (0, i)),
            pl.BlockSpec((block, share), lambda i: (i, 0)),
        ],
        out_specs=[
            pl.BlockSpec((block, share), lambda i: (i, 0)),
            pl.BlockSpec((length, share), lambda i: (0, 0)),
            pl.BlockSpec((length, share), lambda i: (0, 0)),
        ],
        out_shape=[jax.ShapeDtypeStruct((length, share), BF16)] * 3,
        scratch_shapes=[
            pltpu.VMEM((length, block), F32),
            pltpu.VMEM((heads, length, HEAD), F32),
            pltpu.VMEM((heads, length, HEAD), F32),
        ],
        cost_estimate=pl.CostEstimate(
            flops=40 * heads * length * length * HEAD,
            transcendentals=heads * length * length,
            bytes_accessed=8 * length * width,
        ),
        name="attend_back",
    )(qkv, qkv, column, row, logsum, grad)
    return jnp.concatenate(parts, axis=1)


def center(values):
    mean = jnp.mean(values, axis=-1, keepdims=True)
    centred = values - mean
    variance = jnp.mean(centred * centred, axis=-1, keepdims=True)
    rate = lax.rsqrt(variance + EPSILON)
    return centred * rate, rate


def center_back(grad, normal, rate):
    return (
        grad
        - jnp.mean(grad, axis=-1, keepdims=True)
        - normal * jnp.mean(grad * normal, axis=-1, keepdims=True)
    ) * rate


def shards(
    tokens, segments, projections, query_value_bias, out_weight, out_bias, first_gain,
    first_shift, up_weight, up_bias, down_weight, down_bias, second_gain, second_shift, cotangent,
):
    size = lax.axis_size("tensor")
    local_seqs, length, width = tokens.shape
    share = projections.shape[2]
    hidden_share = up_weight.shape[1]
    order = range(size)
    rows = tokens.reshape(-1, width)
    wide = rows.astype(F32)
    valid = (segments != 0).astype(F32).reshape(-1, 1)
    label_rows = [segments[s : s + 1] for s in range(local_seqs)]
    label_columns = [
        jnp.broadcast_to(segments[s][:, None], (length, 128)) for s in range(local_seqs)
    ]

    proj_own = projections.transpose(0, 2, 1).reshape(3 * share, width)
    biases = jnp.concatenate([query_value_bias.reshape(-1), up_bias]).reshape(1, -1)
    biases = gather_shards(biases, size)
    proj = gather_shards(proj_own, size)
    proj[size >> 1], out_weight, up_weight = hold(proj[size >> 1], out_weight, up_weight)
    outs = gather_shards(out_weight, size)
    ups = gather_shards(up_weight, size)
    ups[size >> 1], down_weight = hold(ups[size >> 1], down_weight)
    downs = gather_shards(down_weight, size)

    def pieces(value):
        return [value[s * length : (s + 1) * length] for s in range(local_seqs)]

    def join(values):
        return values[0] if len(values) == 1 else jnp.concatenate(values, axis=0)

    qkv, logsums, contexts = {}, {}, {}
    for r in order:
        flat = biases[r][0]
        bias = jnp.concatenate([flat[:share], jnp.zeros((share,), BF16), flat[share : 2 * share]])
        qkv[r] = (mm(rows, proj[r], NT) + bias.astype(F32)).astype(BF16)
        got = [
            attend(part, label_columns[s], label_rows[s]) for s, part in enumerate(pieces(qkv[r]))
        ]
        contexts[r] = join([g[0] for g in got])
        logsums[r] = [g[1] for g in got]
    context = jnp.concatenate([contexts[r] for r in order], axis=1)
    out_all = jnp.concatenate([outs[r] for r in order], axis=0)
    attention = mm(context, out_all) + out_bias
    normal_one, rate_one = center(wide + attention)
    hidden = normal_one * first_gain + first_shift
    hidden_low = hidden.astype(BF16)
    active, slope = {}, {}
    feed = down_bias
    for r in order:
        up = mm(hidden_low, ups[r]) + biases[r][0, 2 * share :].astype(F32)
        phi = 0.5 * (1.0 + lax.erf(up * 0.7071067811865476))
        active[r] = (up * phi).astype(BF16)
        slope[r] = (phi + up * jnp.exp(-0.5 * up * up) * 0.3989422804014327).astype(BF16)
        feed = feed + mm(active[r], downs[r])
    normal_two, rate_two = center(hidden + feed)
    output = normal_two * second_gain + second_shift
    grad_output = cotangent.reshape(-1, width).astype(F32) * valid
    grad_two = center_back(grad_output * second_gain, normal_two, rate_two)
    grad_two_low = grad_two.astype(BF16)
    low_bits = bits_of(size)
    dp_bits = bits_of(lax.axis_size("dp"))
    last = size - 1

    def fold(group, bit):
        return {
            r: add_low(group[r], swap(group[r | bit], "tensor", bit)) for r in group if not r & bit
        }

    upper = [r for r in order if r & (size >> 1)]
    lower = [r for r in order if not r & (size >> 1)]
    near = low_bits[:-1]
    far = low_bits[-1]

    def near_fold(group):
        for bit in near:
            group = fold(group, bit)
        (key,) = group
        return group[key]

    def far_fold(mine, theirs):
        return add_low(mine, swap(theirs, "tensor", far))

    def down_of(r):
        return mm(active[r], grad_two_low, TN).astype(BF16)

    up_sums, grad_up = {}, {}
    grad_hidden = grad_two

    def up_of(r, grad_hidden):
        up_grad = (mm(grad_two_low, downs[r], NT) * slope[r].astype(F32)).astype(BF16)
        grad_up[r] = mm(hidden_low, up_grad, TN).astype(BF16)
        up_sums[r] = jnp.sum(up_grad.astype(F32), axis=0, keepdims=True)
        return grad_hidden + mm(up_grad, ups[r], NT)

    down_upper = {r: down_of(r) for r in upper}
    grad_two_low, *held = hold(grad_two_low, *down_upper.values())
    down_upper = dict(zip(down_upper, held))
    down_lower = {r: down_of(r) for r in lower}
    down_far = near_fold(down_upper)
    grad_two_low, down_far, *held = hold(grad_two_low, down_far, *down_lower.values())
    down_lower = dict(zip(down_lower, held))
    for r in upper:
        grad_hidden = up_of(r, grad_hidden)
    down_near = near_fold(down_lower)
    held = [grad_up[r] for r in upper]
    grad_two_low, grad_hidden, down_near, *held = hold(
        grad_two_low, grad_hidden, down_near, *held
    )
    up_upper = dict(zip(upper, held))
    up_far = near_fold(up_upper)
    for r in lower:
        grad_hidden = up_of(r, grad_hidden)
    down_chain = Copies(far_fold(down_near, down_far), dp_bits)
    held = [grad_up[r] for r in lower]
    grad_hidden, up_far, down_chain.value, *held = hold(
        grad_hidden, up_far, down_chain.value, *held
    )
    up_lower = dict(zip(lower, held))
    up_near = near_fold(up_lower)

    grad_one = center_back(grad_hidden * first_gain, normal_one, rate_one)
    grad_one_low = grad_one.astype(BF16)
    small = jnp.concatenate(
        [
            jnp.stack(
                [
                    jnp.sum(grad_one, axis=0),
                    jnp.sum(grad_hidden * normal_one, axis=0),
                    jnp.sum(grad_hidden, axis=0),
                    jnp.sum(grad_two, axis=0),
                    jnp.sum(grad_output * normal_two, axis=0),
                    jnp.sum(grad_output, axis=0),
                    jnp.sum(output * output * valid, axis=0),
                    jnp.sum(attention * attention * valid, axis=0),
                    jnp.sum(feed * feed * valid, axis=0),
                    jnp.broadcast_to(jnp.sum(valid) / width, (width,)),
                ]
            ),
            place(up_sums, size).reshape(-1, width),
        ],
        axis=0,
    )
    small_chain = Total(small, ("tensor", "dp"))
    grad_out_all = mm(context, grad_one_low, TN).astype(BF16)
    grad_out = {r: grad_out_all[r * share : (r + 1) * share] for r in order}
    grad_context = mm(grad_one_low, outs[last], NT).astype(BF16)
    grad_context, grad_one_low, grad_out_all, up_near, small_chain.value = hold(
        grad_context, grad_one_low, grad_out_all, up_near, small_chain.value
    )
    grad_out = {r: grad_out_all[r * share : (r + 1) * share] for r in order}
    grad_proj, grad_bias = {}, {}
    stacks = {}
    chains = [down_chain, small_chain]

    def held_with(*values):
        got = hold(*values, *[chain.value for chain in chains])
        for chain, value in zip(chains, got[len(values) :]):
            chain.value = value
        return got[: len(values)]

    walk = upper[::-1] + lower[::-1]
    up_total = out_far = out_near = None
    proj_far = None
    for count, r in enumerate(walk):
        for chain in chains:
            chain.step()
        if count == 0:
            up_total = far_fold(up_near, up_far)
            out_far = near_fold({t: grad_out[t] for t in upper})
            out_near = near_fold({t: grad_out[t] for t in lower})
        if count == len(upper):
            proj_far = near_fold({t: grad_proj[t] for t in upper})
        stacked = join(
            [
                attend_back(part, label_columns[s], label_rows[s], logsums[r][s], grad)
                for s, (part, grad) in enumerate(zip(pieces(qkv[r]), pieces(grad_context)))
            ]
        )
        if count == 0:
            stacked, grad_one_low, up_total, out_far, out_near = held_with(
                stacked, grad_one_low, up_total, out_far, out_near
            )
        elif count == len(upper):
            stacked, grad_one_low, proj_far = held_with(stacked, grad_one_low, proj_far)
        else:
            stacked, grad_one_low = held_with(stacked, grad_one_low)
        for chain in chains:
            chain.step()
        if count == 0:
            out_total = far_fold(out_near, out_far)
        grad_proj[r] = mm(stacked, rows, TN).astype(BF16)
        stacks[r] = stacked
        if count + 1 < size:
            grad_context = mm(grad_one_low, outs[walk[count + 1]], NT).astype(BF16)
            if count == 0:
                chains.append(Copies(jnp.concatenate([up_total, out_total], axis=0), dp_bits))
            grad_context, grad_proj[r] = held_with(grad_context, grad_proj[r])
    proj_total = far_fold(near_fold({t: grad_proj[t] for t in lower}), proj_far)
    total_rows = proj_total.shape[0]
    parts = 2 if total_rows % (2 * lax.axis_size("dp")) == 0 else 1
    cut = total_rows // parts
    halves = [
        Copies(proj_total[n * cut : (n + 1) * cut], dp_bits[n:] + dp_bits[:n])
        for n in range(parts)
    ]
    for r in order:
        sums = jnp.sum(stacks[r].astype(F32), axis=0, keepdims=True)
        grad_bias[r] = jnp.concatenate([sums[:, :share], sums[:, 2 * share :]], axis=1)
    bias_chain = Total(place(grad_bias, size), ("tensor", "dp"))
    grad_input = grad_one
    for r in order:
        grad_input = grad_input + mm(stacks[r], proj[r])
    me = lax.axis_index("tensor")
    total_bias = lax.dynamic_slice_in_dim(bias_chain.finish(), me, 1, 0).reshape(2, share)
    total_down = down_chain.finish()
    total_both = chains[-1].finish()
    total_up, total_out = total_both[:width], total_both[width:]
    total_proj = join([chain.finish() for chain in halves])
    total_proj = total_proj.astype(F32).reshape(3, share, width).transpose(0, 2, 1)
    small = small_chain.finish()
    stats = jnp.sum(small[6:10], axis=1)
    root_means = jnp.sqrt(stats[:3] / (stats[3] * width))
    total_up_bias = lax.dynamic_slice_in_dim(small[10:].reshape(size, hidden_share), me, 1, 0)
    return (
        output.astype(BF16).reshape(tokens.shape),
        grad_input.astype(BF16).reshape(tokens.shape),
        total_proj,
        total_bias,
        total_out.astype(F32),
        small[0],
        small[1],
        small[2],
        total_up.astype(F32),
        total_up_bias.reshape(hidden_share),
        total_down.astype(F32),
        small[3],
        small[4],
        small[5],
        root_means,
    )


def solution(mesh):
    both = P(("dp", "tensor"), None, None)
    column = P(None, "tensor")
    in_specs = (
        both, P(("dp", "tensor"), None), P(None, None, "tensor"), column, P("tensor", None),
        P(), P(), P(), column, P("tensor"), P("tensor", None), P(), P(), P(), both,
    )
    out_specs = (
        both, both, P(None, None, "tensor"), column, P("tensor", None), P(), P(), P(),
        column, P("tensor"), P("tensor", None), P(), P(), P(), P(),
    )
    return jax.shard_map(shards, mesh=mesh, in_specs=in_specs, out_specs=out_specs, check_vma=False)
```

```python
import jax
import jax.numpy as jnp
from jax import lax
from jax.experimental import pallas as pl
from jax.experimental.pallas import tpu as pltpu
from jax.sharding import PartitionSpec as P

HEAD = 64
EPSILON = 1e-06
BLOCK = 256
F32 = jnp.float32
BF16 = jnp.bfloat16


NT = (((1,), (1,)), ((), ()))
NN = (((1,), (0,)), ((), ()))
TN = (((0,), (0,)), ((), ()))


def mm(left, right, dims=NN):
    return lax.dot_general(left, right, dims, preferred_element_type=F32)


def bits_of(size):
    return [1 << b for b in range(size.bit_length() - 1)]


def swap(value, axis, bit):
    size = lax.axis_size(axis)
    return lax.ppermute(value, axis, [(i, i ^ bit) for i in range(size)])


def spread(own, bits, base=0):
    pieces = {base: own}
    for bit in reversed(bits):
        for r in list(pieces):
            pieces[r | bit] = swap(pieces[r], "tensor", bit)
    return pieces


def add_low(left, right):
    return (left.astype(F32) + right.astype(F32)).astype(left.dtype)


def hold(*values):
    return lax.optimization_barrier(values)


class Total:
    def __init__(self, value, axes):
        self.value = value
        self.todo = [(axis, bit) for axis in axes for bit in bits_of(lax.axis_size(axis))]

    def step(self):
        if self.todo:
            axis, bit = self.todo.pop(0)
            self.value = self.value + swap(self.value, axis, bit)

    def finish(self):
        while self.todo:
            self.step()
        return self.value


def place(pieces, size):
    me = lax.axis_index("tensor")
    rows = [pieces[r] for r in range(size)]
    return jnp.concatenate(
        [sum(jnp.where(me ^ r == t, rows[r], 0.0) for r in range(size)) for t in range(size)],
        axis=0,
    )


def attend_kernel(qkv_ref, all_ref, column_ref, row_ref, context_ref, logsum_ref, bias_ref):
    share = context_ref.shape[1]
    heads = share // HEAD
    scale = HEAD ** (-0.5)
    bias_ref[...] = jnp.where(column_ref[:, :1] == row_ref[...], 0.0, -1e30)
    for h in range(heads):
        at = h * HEAD
        queries = qkv_ref[:, at : at + HEAD] * jnp.asarray(scale, BF16)
        keys = all_ref[:, share + at : share + at + HEAD]
        values = all_ref[:, 2 * share + at : 2 * share + at + HEAD]
        scores = mm(keys, queries, NT) + bias_ref[...]
        maximum = jnp.max(scores, axis=0, keepdims=True)
        exponents = jnp.exp(scores - maximum)
        total = jnp.sum(exponents, axis=0, keepdims=True)
        context = mm(values.T, exponents.astype(BF16)) / total
        context_ref[:, at : at + HEAD] = context.T.astype(BF16)
        logsum_ref[h : h + 1, :] = maximum + jnp.log(total)


def attend(qkv, column, row):
    length, width = qkv.shape
    share = width // 3
    heads = share // HEAD
    block = min(BLOCK, length)
    steps = length // block
    return pl.pallas_call(
        attend_kernel,
        grid=(steps,),
        in_specs=[
            pl.BlockSpec((block, width), lambda i: (i, 0)),
            pl.BlockSpec((length, width), lambda i: (0, 0)),
            pl.BlockSpec((length, 128), lambda i: (0, 0)),
            pl.BlockSpec((1, block), lambda i: (0, i)),
        ],
        out_specs=[
            pl.BlockSpec((block, share), lambda i: (i, 0)),
            pl.BlockSpec((heads, block), lambda i: (0, i)),
        ],
        out_shape=[
            jax.ShapeDtypeStruct((length, share), BF16),
            jax.ShapeDtypeStruct((heads, length), F32),
        ],
        scratch_shapes=[pltpu.VMEM((length, block), F32)],
        cost_estimate=pl.CostEstimate(
            flops=16 * heads * length * length * HEAD,
            transcendentals=heads * length * length,
            bytes_accessed=4 * length * width,
        ),
        name="attend",
    )(qkv, qkv, column, row)


def back_kernel(
    qkv_ref, all_ref, column_ref, row_ref, logsum_ref, grad_ref, query_ref, key_ref, value_ref,
    bias_ref, key_sum, value_sum,
):
    share = grad_ref.shape[1]
    heads = share // HEAD
    scale = HEAD ** (-0.5)
    step = pl.program_id(0)
    bias_ref[...] = jnp.where(column_ref[:, :1] == row_ref[...], 0.0, -1e30)

    @pl.when(step == 0)
    def _():
        key_sum[...] = jnp.zeros_like(key_sum)
        value_sum[...] = jnp.zeros_like(value_sum)

    for h in range(heads):
        at = h * HEAD
        queries = qkv_ref[:, at : at + HEAD] * jnp.asarray(scale, BF16)
        keys = all_ref[:, share + at : share + at + HEAD]
        values = all_ref[:, 2 * share + at : 2 * share + at + HEAD]
        grad = grad_ref[:, at : at + HEAD]
        scores = mm(keys, queries, NT) + bias_ref[...]
        weights = jnp.exp(scores - logsum_ref[h : h + 1, :])
        grad_weights = mm(values, grad, NT)
        correction = jnp.sum(grad_weights * weights, axis=0, keepdims=True)
        grad_scores = (weights * (grad_weights - correction)).astype(BF16)
        value_sum[h] += mm(weights.astype(BF16), grad)
        key_sum[h] += mm(grad_scores, queries)
        grad_queries = mm(keys.T, grad_scores) * scale
        query_ref[:, at : at + HEAD] = grad_queries.T.astype(BF16)

    @pl.when(step == pl.num_programs(0) - 1)
    def _():
        for h in range(heads):
            at = h * HEAD
            key_ref[:, at : at + HEAD] = key_sum[h].astype(BF16)
            value_ref[:, at : at + HEAD] = value_sum[h].astype(BF16)


def attend_back(qkv, column, row, logsum, grad):
    length, width = qkv.shape
    share = width // 3
    heads = share // HEAD
    block = min(BLOCK, length)
    steps = length // block
    parts = pl.pallas_call(
        back_kernel,
        grid=(steps,),
        in_specs=[
            pl.BlockSpec((block, width), lambda i: (i, 0)),
            pl.BlockSpec((length, width), lambda i: (0, 0)),
            pl.BlockSpec((length, 128), lambda i: (0, 0)),
            pl.BlockSpec((1, block), lambda i: (0, i)),
            pl.BlockSpec((heads, block), lambda i: (0, i)),
            pl.BlockSpec((block, share), lambda i: (i, 0)),
        ],
        out_specs=[
            pl.BlockSpec((block, share), lambda i: (i, 0)),
            pl.BlockSpec((length, share), lambda i: (0, 0)),
            pl.BlockSpec((length, share), lambda i: (0, 0)),
        ],
        out_shape=[jax.ShapeDtypeStruct((length, share), BF16)] * 3,
        scratch_shapes=[
            pltpu.VMEM((length, block), F32),
            pltpu.VMEM((heads, length, HEAD), F32),
            pltpu.VMEM((heads, length, HEAD), F32),
        ],
        cost_estimate=pl.CostEstimate(
            flops=40 * heads * length * length * HEAD,
            transcendentals=heads * length * length,
            bytes_accessed=8 * length * width,
        ),
        name="attend_back",
    )(qkv, qkv, column, row, logsum, grad)
    return jnp.concatenate(parts, axis=1)


def center(values):
    mean = jnp.mean(values, axis=-1, keepdims=True)
    centred = values - mean
    variance = jnp.mean(centred * centred, axis=-1, keepdims=True)
    rate = lax.rsqrt(variance + EPSILON)
    return centred * rate, rate


def center_back(grad, normal, rate):
    return (
        grad
        - jnp.mean(grad, axis=-1, keepdims=True)
        - normal * jnp.mean(grad * normal, axis=-1, keepdims=True)
    ) * rate


def shards(
    tokens, segments, projections, query_value_bias, out_weight, out_bias, first_gain,
    first_shift, up_weight, up_bias, down_weight, down_bias, second_gain, second_shift, cotangent,
):
    size = lax.axis_size("tensor")
    local_seqs, length, width = tokens.shape
    share = projections.shape[2]
    hidden_share = up_weight.shape[1]
    order = range(size)
    rows = tokens.reshape(-1, width)
    wide = rows.astype(F32)
    valid = (segments != 0).astype(F32).reshape(-1, 1)
    label_rows = [segments[s : s + 1] for s in range(local_seqs)]
    label_columns = [
        jnp.broadcast_to(segments[s][:, None], (length, 128)) for s in range(local_seqs)
    ]

    proj_rows = 3 * share
    bias_rows = -(-(2 * share + hidden_share) // width)
    pad_rows = -(-bias_rows // 16) * 16
    biases = jnp.concatenate([query_value_bias.reshape(-1), up_bias])
    biases = jnp.pad(biases, (0, pad_rows * width - biases.shape[0])).reshape(pad_rows, width)
    proj_own = projections.transpose(0, 2, 1).reshape(proj_rows, width)
    bits = bits_of(size)
    near, far = bits[:-1], bits[-1]
    firsts = spread(jnp.concatenate([proj_own, biases], axis=0), near)
    firsts[far] = swap(firsts[0], "tensor", far)
    out_up = jnp.concatenate([out_weight, up_weight], axis=0)

    def pieces(value):
        return [value[s * length : (s + 1) * length] for s in range(local_seqs)]

    def join(values):
        return values[0] if len(values) == 1 else jnp.concatenate(values, axis=0)

    qkv, logsums, contexts, biases = {}, {}, {}, {}
    for r in order:
        biases[r] = firsts[r][proj_rows:].reshape(1, -1)
        flat = biases[r][0]
        bias = jnp.concatenate([flat[:share], jnp.zeros((share,), BF16), flat[share : 2 * share]])
        qkv[r] = (mm(rows, firsts[r][:proj_rows], NT) + bias.astype(F32)).astype(BF16)
        got = [
            attend(part, label_columns[s], label_rows[s]) for s, part in enumerate(pieces(qkv[r]))
        ]
        contexts[r] = join([g[0] for g in got])
        logsums[r] = [g[1] for g in got]
        if r == 0:
            held = [t for t in firsts if t]
            contexts[0], out_up, down_weight, *got = hold(
                contexts[0], out_up, down_weight, *[firsts[t] for t in held]
            )
            firsts.update(zip(held, got))
            firsts.update(spread(firsts[far], near, far))
            seconds = spread(out_up, near)
            downs = spread(down_weight, near)
            seconds[far] = swap(out_up, "tensor", far)
            downs[far] = swap(down_weight, "tensor", far)
        elif r == size - 2:
            contexts[r], firsts[r + 1], seconds[far] = hold(
                contexts[r], firsts[r + 1], seconds[far]
            )
            seconds.update(spread(seconds[far], near, far))
        elif r + 1 < size:
            contexts[r], firsts[r + 1] = hold(contexts[r], firsts[r + 1])
    outs = {r: seconds[r][:share] for r in order}
    ups = {r: seconds[r][share:] for r in order}
    proj = {r: firsts[r][:proj_rows] for r in order}
    context = jnp.concatenate([contexts[r] for r in order], axis=1)
    out_all = jnp.concatenate([outs[r] for r in order], axis=0)
    attention = mm(context, out_all) + out_bias
    normal_one, rate_one = center(wide + attention)
    hidden = normal_one * first_gain + first_shift
    hidden_low = hidden.astype(BF16)
    active, slope = {}, {}
    feed = down_bias
    for r in order:
        up = mm(hidden_low, ups[r]) + biases[r][0, 2 * share : 2 * share + hidden_share].astype(F32)
        phi = 0.5 * (1.0 + lax.erf(up * 0.7071067811865476))
        active[r] = (up * phi).astype(BF16)
        slope[r] = (phi + up * jnp.exp(-0.5 * up * up) * 0.3989422804014327).astype(BF16)
        feed = feed + mm(active[r], downs[r])
        if r == far - 1:
            feed, hidden_low, downs[far] = hold(feed, hidden_low, downs[far])
            downs.update(spread(downs[far], near, far))
    normal_two, rate_two = center(hidden + feed)
    output = normal_two * second_gain + second_shift
    grad_output = cotangent.reshape(-1, width).astype(F32) * valid
    grad_two = center_back(grad_output * second_gain, normal_two, rate_two)
    grad_two_low = grad_two.astype(BF16)
    upper = [r for r in order if r & far]
    lower = [r for r in order if not r & far]

    def near_fold(group):
        group = dict(group)
        for bit in near:
            sent = [r for r in group if r & bit]
            got = swap(jnp.concatenate([group[r] for r in sent], axis=0), "tensor", bit)
            n = group[sent[0]].shape[0]
            for i, r in enumerate(sent):
                group[r ^ bit] = add_low(group[r ^ bit], got[i * n : (i + 1) * n])
            group = {r: group[r] for r in group if not r & bit}
        return [group[r] for r in sorted(group)]

    def far_fold(mine, theirs):
        return add_low(mine, swap(theirs, "tensor", far))

    def up_of(r, grad_hidden):
        up_grad = (mm(grad_two_low, downs[r], NT) * slope[r].astype(F32)).astype(BF16)
        grad_up[r] = mm(hidden_low, up_grad, TN).astype(BF16)
        up_sums[r] = jnp.sum(up_grad.astype(F32), axis=0, keepdims=True)
        return grad_hidden + mm(up_grad, ups[r], NT)

    def both_fold(group):
        group = dict(group)
        for bit in near:
            sent = [r for r in group if r & bit]
            got = swap(jnp.concatenate([group[r] for r in sent], axis=0), "tensor", bit)
            n = group[sent[0]].shape[0]
            for i, r in enumerate(sent):
                group[r ^ bit] = add_low(group[r ^ bit], got[i * n : (i + 1) * n])
            group = {r: group[r] for r in group if not r & bit}
        return group[0], group[far]

    up_sums, grad_up = {}, {}
    grad_hidden = grad_two
    grad_down = {r: mm(active[r], grad_two_low, TN).astype(BF16) for r in order}
    grad_two_low, *held = hold(grad_two_low, *[grad_down[r] for r in order])
    grad_down = dict(zip(order, held))
    down_near, down_far = both_fold(grad_down)
    for r in upper[:1]:
        grad_hidden = up_of(r, grad_hidden)
    grad_two_low, grad_hidden, down_near, down_far = hold(
        grad_two_low, grad_hidden, down_near, down_far
    )
    for r in upper[1:] + lower:
        grad_hidden = up_of(r, grad_hidden)
    down_total = far_fold(down_near, down_far)
    held = [grad_up[r] for r in order]
    grad_hidden, down_total, *held = hold(grad_hidden, down_total, *held)
    grad_up = dict(zip(order, held))
    total_down = lax.psum(down_total, "dp")

    grad_one = center_back(grad_hidden * first_gain, normal_one, rate_one)
    grad_one_low = grad_one.astype(BF16)
    small = jnp.concatenate(
        [
            jnp.stack(
                [
                    jnp.sum(grad_one, axis=0),
                    jnp.sum(grad_hidden * normal_one, axis=0),
                    jnp.sum(grad_hidden, axis=0),
                    jnp.sum(grad_two, axis=0),
                    jnp.sum(grad_output * normal_two, axis=0),
                    jnp.sum(grad_output, axis=0),
                    jnp.sum(output * output * valid, axis=0),
                    jnp.sum(attention * attention * valid, axis=0),
                    jnp.sum(feed * feed * valid, axis=0),
                    jnp.broadcast_to(jnp.sum(valid) / width, (width,)),
                ]
            ),
            place(up_sums, size).reshape(-1, width),
        ],
        axis=0,
    )
    small_chain = Total(small, ("tensor", "dp"))
    grad_out_all = mm(context, grad_one_low, TN).astype(BF16)
    walk = upper[::-1] + lower[::-1]
    grad_context = mm(grad_one_low, outs[walk[0]], NT).astype(BF16)
    grad_context, grad_one_low, grad_out_all = hold(grad_context, grad_one_low, grad_out_all)
    both = {
        r: jnp.concatenate([grad_up[r], grad_out_all[r * share : (r + 1) * share]], axis=0)
        for r in order
    }
    grad_proj, stacks = {}, {}
    both_near = both_far = both_total = total_both = proj_far = None
    for count, r in enumerate(walk):
        small_chain.step()
        if count == 0:
            both_near, both_far = both_fold(both)
        if count == 1:
            both_total = far_fold(both_near, both_far)
        if count == len(upper):
            (proj_far,) = near_fold({t: grad_proj[t] for t in upper})
        stacked = join(
            [
                attend_back(part, label_columns[s], label_rows[s], logsums[r][s], grad)
                for s, (part, grad) in enumerate(zip(pieces(qkv[r]), pieces(grad_context)))
            ]
        )
        stacked, grad_one_low, small_chain.value = hold(stacked, grad_one_low, small_chain.value)
        if count == 0:
            stacked, both_near, both_far = hold(stacked, both_near, both_far)
        if count == 1:
            stacked, both_total = hold(stacked, both_total)
            both_total, total_down = hold(both_total, total_down)
            total_both = lax.psum(both_total, "dp")
        if count == len(upper):
            stacked, proj_far = hold(stacked, proj_far)
        stacks[r] = stacked
        sums = jnp.sum(stacked.astype(F32), axis=0)
        sums = jnp.concatenate([sums[:share], sums[2 * share :]])
        high = sums.astype(BF16)
        line = jnp.concatenate([high, (sums - high.astype(F32)).astype(BF16)])
        lines = -(-line.shape[0] // width)
        line = jnp.pad(line, (0, 16 * lines * width - line.shape[0])).reshape(16 * lines, width)
        grad_proj[r] = jnp.concatenate([mm(stacked, rows, TN).astype(BF16), line], axis=0)
        if count + 1 < size:
            grad_context = mm(grad_one_low, outs[walk[count + 1]], NT).astype(BF16)
            grad_context, grad_proj[r] = hold(grad_context, grad_proj[r])
    (proj_near,) = near_fold({t: grad_proj[t] for t in lower})
    proj_total = far_fold(proj_near, proj_far)
    proj_total, total_both = hold(proj_total, total_both)
    total_proj = lax.psum(proj_total, "dp")
    grad_input = grad_one
    for r in order:
        grad_input = grad_input + mm(stacks[r], proj[r])
    total_up, total_out = total_both[:width], total_both[width:]
    line = total_proj[proj_rows:].astype(F32).reshape(-1)
    total_bias = (line[: 2 * share] + line[2 * share : 4 * share]).reshape(2, share)
    total_proj = total_proj[:proj_rows].astype(F32).reshape(3, share, width).transpose(0, 2, 1)
    small = small_chain.finish()
    stats = jnp.sum(small[6:10], axis=1)
    root_means = jnp.sqrt(stats[:3] / (stats[3] * width))
    me = lax.axis_index("tensor")
    total_up_bias = lax.dynamic_slice_in_dim(small[10:].reshape(size, hidden_share), me, 1, 0)
    return (
        output.astype(BF16).reshape(tokens.shape),
        grad_input.astype(BF16).reshape(tokens.shape),
        total_proj,
        total_bias,
        total_out.astype(F32),
        small[0],
        small[1],
        small[2],
        total_up.astype(F32),
        total_up_bias.reshape(hidden_share),
        total_down.astype(F32),
        small[3],
        small[4],
        small[5],
        root_means,
    )


def solution(mesh):
    both = P(("dp", "tensor"), None, None)
    column = P(None, "tensor")
    in_specs = (
        both, P(("dp", "tensor"), None), P(None, None, "tensor"), column, P("tensor", None),
        P(), P(), P(), column, P("tensor"), P("tensor", None), P(), P(), P(), both,
    )
    out_specs = (
        both, both, P(None, None, "tensor"), column, P("tensor", None), P(), P(), P(),
        column, P("tensor"), P("tensor", None), P(), P(), P(), P(),
    )
    return jax.shard_map(shards, mesh=mesh, in_specs=in_specs, out_specs=out_specs, check_vma=False)
```

```python
import jax
import jax.numpy as jnp
from jax import lax
from jax.experimental import pallas as pl
from jax.experimental.pallas import tpu as pltpu
from jax.sharding import PartitionSpec as P

HEAD = 64
EPSILON = 1e-06
BLOCK = 256
F32 = jnp.float32
BF16 = jnp.bfloat16


NT = (((1,), (1,)), ((), ()))
NN = (((1,), (0,)), ((), ()))
TN = (((0,), (0,)), ((), ()))


def mm(left, right, dims=NN):
    return lax.dot_general(left, right, dims, preferred_element_type=F32)


def bits_of(size):
    return [1 << b for b in range(size.bit_length() - 1)]


def swap(value, axis, bit):
    size = lax.axis_size(axis)
    return lax.ppermute(value, axis, [(i, i ^ bit) for i in range(size)])


def spread(own, bits, base=0):
    pieces = {base: own}
    for bit in reversed(bits):
        for r in list(pieces):
            pieces[r | bit] = swap(pieces[r], "tensor", bit)
    return pieces


def add_low(left, right):
    return (left.astype(F32) + right.astype(F32)).astype(left.dtype)


def hold(*values):
    return lax.optimization_barrier(values)


class Copies:
    def __init__(self, value, bits):
        self.value = value
        self.todo, halved, count = [], [], value.shape[0]
        for bit in bits:
            if count % 2 or bit == bits[-1]:
                self.todo.append(("whole", bit))
            else:
                self.todo.append(("halve", bit))
                halved.append(bit)
                count //= 2
        self.todo += [("join", bit) for bit in reversed(halved)]

    def step(self):
        if not self.todo:
            return
        kind, bit = self.todo.pop(0)
        high = (lax.axis_index("dp") & bit) != 0
        value = self.value
        if kind == "halve":
            half = value.shape[0] // 2
            low_part, high_part = value[:half], value[half:]
            sent = jnp.where(high, low_part, high_part)
            kept = jnp.where(high, high_part, low_part)
            self.value = add_low(kept, swap(sent, "dp", bit))
        elif kind == "whole":
            self.value = add_low(value, swap(value, "dp", bit))
        else:
            other = swap(value, "dp", bit)
            self.value = jnp.concatenate(
                [jnp.where(high, other, value), jnp.where(high, value, other)], axis=0
            )

    def finish(self):
        while self.todo:
            self.step()
        return self.value


class Total:
    def __init__(self, value, axes):
        self.value = value
        self.todo = [(axis, bit) for axis in axes for bit in bits_of(lax.axis_size(axis))]

    def step(self):
        if self.todo:
            axis, bit = self.todo.pop(0)
            self.value = self.value + swap(self.value, axis, bit)

    def finish(self):
        while self.todo:
            self.step()
        return self.value


def place(pieces, size):
    me = lax.axis_index("tensor")
    rows = [pieces[r] for r in range(size)]
    return jnp.concatenate(
        [sum(jnp.where(me ^ r == t, rows[r], 0.0) for r in range(size)) for t in range(size)],
        axis=0,
    )


def attend_kernel(qkv_ref, all_ref, column_ref, row_ref, context_ref, logsum_ref, bias_ref):
    share = context_ref.shape[1]
    heads = share // HEAD
    scale = HEAD ** (-0.5)
    bias_ref[...] = jnp.where(column_ref[:, :1] == row_ref[...], 0.0, -1e30)
    for h in range(heads):
        at = h * HEAD
        queries = qkv_ref[:, at : at + HEAD] * jnp.asarray(scale, BF16)
        keys = all_ref[:, share + at : share + at + HEAD]
        values = all_ref[:, 2 * share + at : 2 * share + at + HEAD]
        scores = mm(keys, queries, NT) + bias_ref[...]
        maximum = jnp.max(scores, axis=0, keepdims=True)
        exponents = jnp.exp(scores - maximum)
        total = jnp.sum(exponents, axis=0, keepdims=True)
        context = mm(values.T, exponents.astype(BF16)) / total
        context_ref[:, at : at + HEAD] = context.T.astype(BF16)
        logsum_ref[h : h + 1, :] = maximum + jnp.log(total)


def attend(qkv, column, row):
    length, width = qkv.shape
    share = width // 3
    heads = share // HEAD
    block = min(BLOCK, length)
    steps = length // block
    return pl.pallas_call(
        attend_kernel,
        grid=(steps,),
        in_specs=[
            pl.BlockSpec((block, width), lambda i: (i, 0)),
            pl.BlockSpec((length, width), lambda i: (0, 0)),
            pl.BlockSpec((length, 128), lambda i: (0, 0)),
            pl.BlockSpec((1, block), lambda i: (0, i)),
        ],
        out_specs=[
            pl.BlockSpec((block, share), lambda i: (i, 0)),
            pl.BlockSpec((heads, block), lambda i: (0, i)),
        ],
        out_shape=[
            jax.ShapeDtypeStruct((length, share), BF16),
            jax.ShapeDtypeStruct((heads, length), F32),
        ],
        scratch_shapes=[pltpu.VMEM((length, block), F32)],
        cost_estimate=pl.CostEstimate(
            flops=16 * heads * length * length * HEAD,
            transcendentals=heads * length * length,
            bytes_accessed=4 * length * width,
        ),
        name="attend",
    )(qkv, qkv, column, row)


def back_kernel(
    qkv_ref, all_ref, column_ref, row_ref, logsum_ref, grad_ref, query_ref, key_ref, value_ref,
    bias_ref, key_sum, value_sum,
):
    share = grad_ref.shape[1]
    heads = share // HEAD
    scale = HEAD ** (-0.5)
    step = pl.program_id(0)
    bias_ref[...] = jnp.where(column_ref[:, :1] == row_ref[...], 0.0, -1e30)

    @pl.when(step == 0)
    def _():
        key_sum[...] = jnp.zeros_like(key_sum)
        value_sum[...] = jnp.zeros_like(value_sum)

    for h in range(heads):
        at = h * HEAD
        queries = qkv_ref[:, at : at + HEAD] * jnp.asarray(scale, BF16)
        keys = all_ref[:, share + at : share + at + HEAD]
        values = all_ref[:, 2 * share + at : 2 * share + at + HEAD]
        grad = grad_ref[:, at : at + HEAD]
        scores = mm(keys, queries, NT) + bias_ref[...]
        weights = jnp.exp(scores - logsum_ref[h : h + 1, :])
        grad_weights = mm(values, grad, NT)
        correction = jnp.sum(grad_weights * weights, axis=0, keepdims=True)
        grad_scores = (weights * (grad_weights - correction)).astype(BF16)
        value_sum[h] += mm(weights.astype(BF16), grad)
        key_sum[h] += mm(grad_scores, queries)
        grad_queries = mm(keys.T, grad_scores) * scale
        query_ref[:, at : at + HEAD] = grad_queries.T.astype(BF16)

    @pl.when(step == pl.num_programs(0) - 1)
    def _():
        for h in range(heads):
            at = h * HEAD
            key_ref[:, at : at + HEAD] = key_sum[h].astype(BF16)
            value_ref[:, at : at + HEAD] = value_sum[h].astype(BF16)


def attend_back(qkv, column, row, logsum, grad):
    length, width = qkv.shape
    share = width // 3
    heads = share // HEAD
    block = min(BLOCK, length)
    steps = length // block
    parts = pl.pallas_call(
        back_kernel,
        grid=(steps,),
        in_specs=[
            pl.BlockSpec((block, width), lambda i: (i, 0)),
            pl.BlockSpec((length, width), lambda i: (0, 0)),
            pl.BlockSpec((length, 128), lambda i: (0, 0)),
            pl.BlockSpec((1, block), lambda i: (0, i)),
            pl.BlockSpec((heads, block), lambda i: (0, i)),
            pl.BlockSpec((block, share), lambda i: (i, 0)),
        ],
        out_specs=[
            pl.BlockSpec((block, share), lambda i: (i, 0)),
            pl.BlockSpec((length, share), lambda i: (0, 0)),
            pl.BlockSpec((length, share), lambda i: (0, 0)),
        ],
        out_shape=[jax.ShapeDtypeStruct((length, share), BF16)] * 3,
        scratch_shapes=[
            pltpu.VMEM((length, block), F32),
            pltpu.VMEM((heads, length, HEAD), F32),
            pltpu.VMEM((heads, length, HEAD), F32),
        ],
        cost_estimate=pl.CostEstimate(
            flops=40 * heads * length * length * HEAD,
            transcendentals=heads * length * length,
            bytes_accessed=8 * length * width,
        ),
        name="attend_back",
    )(qkv, qkv, column, row, logsum, grad)
    return jnp.concatenate(parts, axis=1)


def center(values):
    mean = jnp.mean(values, axis=-1, keepdims=True)
    centred = values - mean
    variance = jnp.mean(centred * centred, axis=-1, keepdims=True)
    rate = lax.rsqrt(variance + EPSILON)
    return centred * rate, rate


def center_back(grad, normal, rate):
    return (
        grad
        - jnp.mean(grad, axis=-1, keepdims=True)
        - normal * jnp.mean(grad * normal, axis=-1, keepdims=True)
    ) * rate


def shards(
    tokens, segments, projections, query_value_bias, out_weight, out_bias, first_gain,
    first_shift, up_weight, up_bias, down_weight, down_bias, second_gain, second_shift, cotangent,
):
    size = lax.axis_size("tensor")
    local_seqs, length, width = tokens.shape
    share = projections.shape[2]
    hidden_share = up_weight.shape[1]
    order = range(size)
    rows = tokens.reshape(-1, width)
    wide = rows.astype(F32)
    valid = (segments != 0).astype(F32).reshape(-1, 1)
    label_rows = [segments[s : s + 1] for s in range(local_seqs)]
    label_columns = [
        jnp.broadcast_to(segments[s][:, None], (length, 128)) for s in range(local_seqs)
    ]

    proj_rows = 3 * share
    bias_rows = -(-(2 * share + hidden_share) // width)
    pad_rows = -(-bias_rows // 16) * 16
    biases = jnp.concatenate([query_value_bias.reshape(-1), up_bias])
    biases = jnp.pad(biases, (0, pad_rows * width - biases.shape[0])).reshape(pad_rows, width)
    proj_own = projections.transpose(0, 2, 1).reshape(proj_rows, width)
    bits = bits_of(size)
    near, far = bits[:-1], bits[-1]
    firsts = spread(jnp.concatenate([proj_own, biases], axis=0), near)
    firsts[far] = swap(firsts[0], "tensor", far)
    out_up = jnp.concatenate([out_weight, up_weight], axis=0)

    def pieces(value):
        return [value[s * length : (s + 1) * length] for s in range(local_seqs)]

    def join(values):
        return values[0] if len(values) == 1 else jnp.concatenate(values, axis=0)

    qkv, logsums, contexts, biases = {}, {}, {}, {}
    for r in order:
        biases[r] = firsts[r][proj_rows:].reshape(1, -1)
        flat = biases[r][0]
        bias = jnp.concatenate([flat[:share], jnp.zeros((share,), BF16), flat[share : 2 * share]])
        qkv[r] = (mm(rows, firsts[r][:proj_rows], NT) + bias.astype(F32)).astype(BF16)
        got = [
            attend(part, label_columns[s], label_rows[s]) for s, part in enumerate(pieces(qkv[r]))
        ]
        contexts[r] = join([g[0] for g in got])
        logsums[r] = [g[1] for g in got]
        if r == 0:
            held = [t for t in firsts if t]
            contexts[0], out_up, down_weight, *got = hold(
                contexts[0], out_up, down_weight, *[firsts[t] for t in held]
            )
            firsts.update(zip(held, got))
            firsts.update(spread(firsts[far], near, far))
            seconds = spread(out_up, near)
            downs = spread(down_weight, near)
            seconds[far] = swap(out_up, "tensor", far)
            downs[far] = swap(down_weight, "tensor", far)
        elif r == size - 2:
            contexts[r], firsts[r + 1], seconds[far] = hold(
                contexts[r], firsts[r + 1], seconds[far]
            )
            seconds.update(spread(seconds[far], near, far))
        elif r + 1 < size:
            contexts[r], firsts[r + 1] = hold(contexts[r], firsts[r + 1])
    outs = {r: seconds[r][:share] for r in order}
    ups = {r: seconds[r][share:] for r in order}
    proj = {r: firsts[r][:proj_rows] for r in order}
    context = jnp.concatenate([contexts[r] for r in order], axis=1)
    out_all = jnp.concatenate([outs[r] for r in order], axis=0)
    attention = mm(context, out_all) + out_bias
    normal_one, rate_one = center(wide + attention)
    hidden = normal_one * first_gain + first_shift
    hidden_low = hidden.astype(BF16)
    active, slope = {}, {}
    feed = down_bias
    for r in order:
        up = mm(hidden_low, ups[r]) + biases[r][0, 2 * share : 2 * share + hidden_share].astype(F32)
        phi = 0.5 * (1.0 + lax.erf(up * 0.7071067811865476))
        active[r] = (up * phi).astype(BF16)
        slope[r] = (phi + up * jnp.exp(-0.5 * up * up) * 0.3989422804014327).astype(BF16)
        feed = feed + mm(active[r], downs[r])
        if r == far - 1:
            feed, hidden_low, downs[far] = hold(feed, hidden_low, downs[far])
            downs.update(spread(downs[far], near, far))
    normal_two, rate_two = center(hidden + feed)
    output = normal_two * second_gain + second_shift
    grad_output = cotangent.reshape(-1, width).astype(F32) * valid
    grad_two = center_back(grad_output * second_gain, normal_two, rate_two)
    grad_two_low = grad_two.astype(BF16)
    upper = [r for r in order if r & far]
    lower = [r for r in order if not r & far]

    def near_fold(group):
        group = dict(group)
        for bit in near:
            sent = [r for r in group if r & bit]
            got = swap(jnp.concatenate([group[r] for r in sent], axis=0), "tensor", bit)
            n = group[sent[0]].shape[0]
            for i, r in enumerate(sent):
                group[r ^ bit] = add_low(group[r ^ bit], got[i * n : (i + 1) * n])
            group = {r: group[r] for r in group if not r & bit}
        return [group[r] for r in sorted(group)]

    def far_fold(mine, theirs):
        return add_low(mine, swap(theirs, "tensor", far))

    def up_of(r, grad_hidden):
        up_grad = (mm(grad_two_low, downs[r], NT) * slope[r].astype(F32)).astype(BF16)
        grad_up[r] = mm(hidden_low, up_grad, TN).astype(BF16)
        up_sums[r] = jnp.sum(up_grad.astype(F32), axis=0, keepdims=True)
        return grad_hidden + mm(up_grad, ups[r], NT)

    def both_fold(group):
        group = dict(group)
        for bit in near:
            sent = [r for r in group if r & bit]
            got = swap(jnp.concatenate([group[r] for r in sent], axis=0), "tensor", bit)
            n = group[sent[0]].shape[0]
            for i, r in enumerate(sent):
                group[r ^ bit] = add_low(group[r ^ bit], got[i * n : (i + 1) * n])
            group = {r: group[r] for r in group if not r & bit}
        return group[0], group[far]

    dp_bits = bits_of(lax.axis_size("dp"))
    up_sums, grad_up = {}, {}
    grad_hidden = grad_two
    grad_down = {r: mm(active[r], grad_two_low, TN).astype(BF16) for r in order}
    grad_two_low, *held = hold(grad_two_low, *[grad_down[r] for r in order])
    grad_down = dict(zip(order, held))
    down_near, down_far = both_fold(grad_down)
    for r in upper:
        grad_hidden = up_of(r, grad_hidden)
    grad_two_low, grad_hidden, down_near, down_far, *held = hold(
        grad_two_low, grad_hidden, down_near, down_far, *[grad_up[r] for r in upper]
    )
    (up_far,) = near_fold(dict(zip(upper, held)))
    for r in lower:
        grad_hidden = up_of(r, grad_hidden)
    down_total = far_fold(down_near, down_far)
    grad_hidden, down_total, up_far, *held = hold(
        grad_hidden, down_total, up_far, *[grad_up[r] for r in lower]
    )
    (up_near,) = near_fold(dict(zip(lower, held)))
    up_total = far_fold(up_near, up_far)
    down_chain = Copies(down_total, dp_bits)
    down_chain.step()

    grad_one = center_back(grad_hidden * first_gain, normal_one, rate_one)
    grad_one_low = grad_one.astype(BF16)
    small = jnp.concatenate(
        [
            jnp.stack(
                [
                    jnp.sum(grad_one, axis=0),
                    jnp.sum(grad_hidden * normal_one, axis=0),
                    jnp.sum(grad_hidden, axis=0),
                    jnp.sum(grad_two, axis=0),
                    jnp.sum(grad_output * normal_two, axis=0),
                    jnp.sum(grad_output, axis=0),
                    jnp.sum(output * output * valid, axis=0),
                    jnp.sum(attention * attention * valid, axis=0),
                    jnp.sum(feed * feed * valid, axis=0),
                    jnp.broadcast_to(jnp.sum(valid) / width, (width,)),
                ]
            ),
            place(up_sums, size).reshape(-1, width),
        ],
        axis=0,
    )
    small_chain = Total(small, ("tensor", "dp"))
    grad_out_all = mm(context, grad_one_low, TN).astype(BF16)
    walk = upper[::-1] + lower[::-1]
    grad_context = mm(grad_one_low, outs[walk[0]], NT).astype(BF16)
    grad_context, grad_one_low, grad_out_all = hold(grad_context, grad_one_low, grad_out_all)
    grad_out = {r: grad_out_all[r * share : (r + 1) * share] for r in order}
    grad_proj, stacks = {}, {}
    chains = [down_chain, small_chain]
    out_near = out_far = out_total = proj_far = None

    def held_with(*values):
        got = hold(*values, *[chain.value for chain in chains])
        for chain, value in zip(chains, got[len(values) :]):
            chain.value = value
        return got[: len(values)]

    for count, r in enumerate(walk):
        if count == 0:
            out_near, out_far = both_fold(grad_out)
            small_chain.step()
        else:
            for chain in chains:
                chain.step()
        if count == len(upper):
            (proj_far,) = near_fold({t: grad_proj[t] for t in upper})
        stacked = join(
            [
                attend_back(part, label_columns[s], label_rows[s], logsums[r][s], grad)
                for s, (part, grad) in enumerate(zip(pieces(qkv[r]), pieces(grad_context)))
            ]
        )
        stacked, grad_one_low = held_with(stacked, grad_one_low)
        if count == 0:
            stacked, out_near, out_far = hold(stacked, out_near, out_far)
        if count == len(upper):
            stacked, proj_far = hold(stacked, proj_far)
        for chain in chains:
            chain.step()
        if count == 0:
            out_total = far_fold(out_near, out_far)
        stacks[r] = stacked
        sums = jnp.sum(stacked.astype(F32), axis=0)
        sums = jnp.concatenate([sums[:share], sums[2 * share :]])
        high = sums.astype(BF16)
        line = jnp.concatenate([high, (sums - high.astype(F32)).astype(BF16)])
        lines = -(-line.shape[0] // width)
        line = jnp.pad(line, (0, 16 * lines * width - line.shape[0])).reshape(16 * lines, width)
        grad_proj[r] = jnp.concatenate([mm(stacked, rows, TN).astype(BF16), line], axis=0)
        if count + 1 < size:
            grad_context = mm(grad_one_low, outs[walk[count + 1]], NT).astype(BF16)
            if count == 0:
                both = jnp.concatenate([up_total, out_total], axis=0)
                grad_context, both = hold(grad_context, both)
                both_chain = Copies(both, dp_bits)
            grad_context, grad_proj[r] = held_with(grad_context, grad_proj[r])
            if count == 0:
                chains.append(both_chain)
    (proj_near,) = near_fold({t: grad_proj[t] for t in lower})
    proj_total = far_fold(proj_near, proj_far)
    total_rows = proj_total.shape[0]
    parts = 2 if total_rows % (2 * lax.axis_size("dp")) == 0 else 1
    cut = total_rows // parts
    halves = [
        Copies(proj_total[n * cut : (n + 1) * cut], dp_bits[n:] + dp_bits[:n])
        for n in range(parts)
    ]
    for chain in halves:
        chain.step()
    fresh, *got = hold(stacks[walk[-1]], *[chain.value for chain in halves])
    stacks[walk[-1]] = fresh
    for chain, value in zip(halves, got):
        chain.value = value
    total_proj = join([chain.finish() for chain in halves])
    total_down = down_chain.finish()
    total_both = both_chain.finish()
    grad_input = grad_one
    for r in walk:
        grad_input = grad_input + mm(stacks[r], proj[r])
    total_up, total_out = total_both[:width], total_both[width:]
    line = total_proj[proj_rows:].astype(F32).reshape(-1)
    total_bias = (line[: 2 * share] + line[2 * share : 4 * share]).reshape(2, share)
    total_proj = total_proj[:proj_rows].astype(F32).reshape(3, share, width).transpose(0, 2, 1)
    small = small_chain.finish()
    stats = jnp.sum(small[6:10], axis=1)
    root_means = jnp.sqrt(stats[:3] / (stats[3] * width))
    me = lax.axis_index("tensor")
    total_up_bias = lax.dynamic_slice_in_dim(small[10:].reshape(size, hidden_share), me, 1, 0)
    return (
        output.astype(BF16).reshape(tokens.shape),
        grad_input.astype(BF16).reshape(tokens.shape),
        total_proj,
        total_bias,
        total_out.astype(F32),
        small[0],
        small[1],
        small[2],
        total_up.astype(F32),
        total_up_bias.reshape(hidden_share),
        total_down.astype(F32),
        small[3],
        small[4],
        small[5],
        root_means,
    )


def solution(mesh):
    both = P(("dp", "tensor"), None, None)
    column = P(None, "tensor")
    in_specs = (
        both, P(("dp", "tensor"), None), P(None, None, "tensor"), column, P("tensor", None),
        P(), P(), P(), column, P("tensor"), P("tensor", None), P(), P(), P(), both,
    )
    out_specs = (
        both, both, P(None, None, "tensor"), column, P("tensor", None), P(), P(), P(),
        column, P("tensor"), P("tensor", None), P(), P(), P(), P(),
    )
    return jax.shard_map(shards, mesh=mesh, in_specs=in_specs, out_specs=out_specs, check_vma=False)
```

```python
import jax
import jax.numpy as jnp
from jax import lax
from jax.experimental import pallas as pl
from jax.experimental.pallas import tpu as pltpu
from jax.sharding import PartitionSpec as P


HEAD = 64
EPSILON = 1e-06
BLOCK = 256
F32 = jnp.float32
BF16 = jnp.bfloat16


NT = (((1,), (1,)), ((), ()))
NN = (((1,), (0,)), ((), ()))
TN = (((0,), (0,)), ((), ()))


def mm(left, right, dims=NN):
    return lax.dot_general(left, right, dims, preferred_element_type=F32)


def bits_of(size):
    return [1 << b for b in range(size.bit_length() - 1)]


def swap(value, axis, bit):
    size = lax.axis_size(axis)
    return lax.ppermute(value, axis, [(i, i ^ bit) for i in range(size)])


def spread(own, bits, base=0):
    pieces = {base: own}
    for bit in reversed(bits):
        for r in list(pieces):
            pieces[r | bit] = swap(pieces[r], "tensor", bit)
    return pieces


def add_low(left, right):
    return (left.astype(F32) + right.astype(F32)).astype(left.dtype)


def hold(*values):
    return lax.optimization_barrier(values)


class Copies:
    def __init__(self, value, bits):
        self.value = value
        self.todo, halved, count = [], [], value.shape[0]
        for bit in bits:
            if count % 2 or bit == bits[-1]:
                self.todo.append(("whole", bit))
            else:
                self.todo.append(("halve", bit))
                halved.append(bit)
                count //= 2
        self.todo += [("join", bit) for bit in reversed(halved)]

    def step(self):
        if not self.todo:
            return
        kind, bit = self.todo.pop(0)
        high = (lax.axis_index("dp") & bit) != 0
        value = self.value
        if kind == "halve":
            half = value.shape[0] // 2
            low_part, high_part = value[:half], value[half:]
            sent = jnp.where(high, low_part, high_part)
            kept = jnp.where(high, high_part, low_part)
            self.value = add_low(kept, swap(sent, "dp", bit))
        elif kind == "whole":
            self.value = add_low(value, swap(value, "dp", bit))
        else:
            other = swap(value, "dp", bit)
            self.value = jnp.concatenate(
                [jnp.where(high, other, value), jnp.where(high, value, other)], axis=0
            )

    def finish(self):
        while self.todo:
            self.step()
        return self.value


class Total:
    def __init__(self, value, axes):
        self.value = value
        self.todo = [(axis, bit) for axis in axes for bit in bits_of(lax.axis_size(axis))]

    def step(self):
        if self.todo:
            axis, bit = self.todo.pop(0)
            self.value = self.value + swap(self.value, axis, bit)

    def finish(self):
        while self.todo:
            self.step()
        return self.value


def place(pieces, size):
    me = lax.axis_index("tensor")
    rows = [pieces[r] for r in range(size)]
    return jnp.concatenate(
        [sum(jnp.where(me ^ r == t, rows[r], 0.0) for r in range(size)) for t in range(size)],
        axis=0,
    )


def attend_kernel(qkv_ref, all_ref, column_ref, row_ref, context_ref, logsum_ref, bias_ref):
    share = context_ref.shape[1]
    heads = share // HEAD
    scale = HEAD ** (-0.5)
    bias_ref[...] = jnp.where(column_ref[:, :1] == row_ref[...], 0.0, -1e30)
    for h in range(heads):
        at = h * HEAD
        queries = qkv_ref[:, at : at + HEAD] * jnp.asarray(scale, BF16)
        keys = all_ref[:, share + at : share + at + HEAD]
        values = all_ref[:, 2 * share + at : 2 * share + at + HEAD]
        scores = mm(keys, queries, NT) + bias_ref[...]
        maximum = jnp.max(scores, axis=0, keepdims=True)
        exponents = jnp.exp(scores - maximum)
        total = jnp.sum(exponents, axis=0, keepdims=True)
        context = mm(values.T, exponents.astype(BF16)) / total
        context_ref[:, at : at + HEAD] = context.T.astype(BF16)
        logsum_ref[h : h + 1, :] = maximum + jnp.log(total)


def attend(qkv, column, row):
    length, width = qkv.shape
    share = width // 3
    heads = share // HEAD
    block = min(BLOCK, length)
    steps = length // block
    return pl.pallas_call(
        attend_kernel,
        grid=(steps,),
        in_specs=[
            pl.BlockSpec((block, width), lambda i: (i, 0)),
            pl.BlockSpec((length, width), lambda i: (0, 0)),
            pl.BlockSpec((length, 128), lambda i: (0, 0)),
            pl.BlockSpec((1, block), lambda i: (0, i)),
        ],
        out_specs=[
            pl.BlockSpec((block, share), lambda i: (i, 0)),
            pl.BlockSpec((heads, block), lambda i: (0, i)),
        ],
        out_shape=[
            jax.ShapeDtypeStruct((length, share), BF16),
            jax.ShapeDtypeStruct((heads, length), F32),
        ],
        scratch_shapes=[pltpu.VMEM((length, block), F32)],
        cost_estimate=pl.CostEstimate(
            flops=16 * heads * length * length * HEAD,
            transcendentals=heads * length * length,
            bytes_accessed=4 * length * width,
        ),
        name="attend",
    )(qkv, qkv, column, row)


def back_kernel(
    qkv_ref, all_ref, column_ref, row_ref, logsum_ref, grad_ref, query_ref, key_ref, value_ref,
    bias_ref, key_sum, value_sum,
):
    share = grad_ref.shape[1]
    heads = share // HEAD
    scale = HEAD ** (-0.5)
    step = pl.program_id(0)
    bias_ref[...] = jnp.where(column_ref[:, :1] == row_ref[...], 0.0, -1e30)

    @pl.when(step == 0)
    def _():
        key_sum[...] = jnp.zeros_like(key_sum)
        value_sum[...] = jnp.zeros_like(value_sum)

    for h in range(heads):
        at = h * HEAD
        queries = qkv_ref[:, at : at + HEAD] * jnp.asarray(scale, BF16)
        keys = all_ref[:, share + at : share + at + HEAD]
        values = all_ref[:, 2 * share + at : 2 * share + at + HEAD]
        grad = grad_ref[:, at : at + HEAD]
        scores = mm(keys, queries, NT) + bias_ref[...]
        weights = jnp.exp(scores - logsum_ref[h : h + 1, :])
        grad_weights = mm(values, grad, NT)
        correction = jnp.sum(grad_weights * weights, axis=0, keepdims=True)
        grad_scores = (weights * (grad_weights - correction)).astype(BF16)
        value_sum[h] += mm(weights.astype(BF16), grad)
        key_sum[h] += mm(grad_scores, queries)
        grad_queries = mm(keys.T, grad_scores) * scale
        query_ref[:, at : at + HEAD] = grad_queries.T.astype(BF16)

    @pl.when(step == pl.num_programs(0) - 1)
    def _():
        for h in range(heads):
            at = h * HEAD
            key_ref[:, at : at + HEAD] = key_sum[h].astype(BF16)
            value_ref[:, at : at + HEAD] = value_sum[h].astype(BF16)


def attend_back(qkv, column, row, logsum, grad):
    length, width = qkv.shape
    share = width // 3
    heads = share // HEAD
    block = min(BLOCK, length)
    steps = length // block
    parts = pl.pallas_call(
        back_kernel,
        grid=(steps,),
        in_specs=[
            pl.BlockSpec((block, width), lambda i: (i, 0)),
            pl.BlockSpec((length, width), lambda i: (0, 0)),
            pl.BlockSpec((length, 128), lambda i: (0, 0)),
            pl.BlockSpec((1, block), lambda i: (0, i)),
            pl.BlockSpec((heads, block), lambda i: (0, i)),
            pl.BlockSpec((block, share), lambda i: (i, 0)),
        ],
        out_specs=[
            pl.BlockSpec((block, share), lambda i: (i, 0)),
            pl.BlockSpec((length, share), lambda i: (0, 0)),
            pl.BlockSpec((length, share), lambda i: (0, 0)),
        ],
        out_shape=[jax.ShapeDtypeStruct((length, share), BF16)] * 3,
        scratch_shapes=[
            pltpu.VMEM((length, block), F32),
            pltpu.VMEM((heads, length, HEAD), F32),
            pltpu.VMEM((heads, length, HEAD), F32),
        ],
        cost_estimate=pl.CostEstimate(
            flops=40 * heads * length * length * HEAD,
            transcendentals=heads * length * length,
            bytes_accessed=8 * length * width,
        ),
        name="attend_back",
    )(qkv, qkv, column, row, logsum, grad)
    return jnp.concatenate(parts, axis=1)


def center(values):
    mean = jnp.mean(values, axis=-1, keepdims=True)
    centred = values - mean
    variance = jnp.mean(centred * centred, axis=-1, keepdims=True)
    rate = lax.rsqrt(variance + EPSILON)
    return centred * rate, rate


def center_back(grad, normal, rate):
    return (
        grad
        - jnp.mean(grad, axis=-1, keepdims=True)
        - normal * jnp.mean(grad * normal, axis=-1, keepdims=True)
    ) * rate


def shards(
    tokens, segments, projections, query_value_bias, out_weight, out_bias, first_gain,
    first_shift, up_weight, up_bias, down_weight, down_bias, second_gain, second_shift, cotangent,
):
    size = lax.axis_size("tensor")
    local_seqs, length, width = tokens.shape
    share = projections.shape[2]
    hidden_share = up_weight.shape[1]
    order = range(size)
    rows = tokens.reshape(-1, width)
    wide = rows.astype(F32)
    valid = (segments != 0).astype(F32).reshape(-1, 1)
    label_rows = [segments[s : s + 1] for s in range(local_seqs)]
    label_columns = [
        jnp.broadcast_to(segments[s][:, None], (length, 128)) for s in range(local_seqs)
    ]

    proj_rows = 3 * share
    bias_rows = -(-(2 * share + hidden_share) // width)
    pad_rows = -(-bias_rows // 16) * 16
    biases = jnp.concatenate([query_value_bias.reshape(-1), up_bias])
    biases = jnp.pad(biases, (0, pad_rows * width - biases.shape[0])).reshape(pad_rows, width)
    proj_own = projections.transpose(0, 2, 1).reshape(proj_rows, width)
    bits = bits_of(size)
    near, far = bits[:-1], bits[-1]
    firsts = spread(jnp.concatenate([proj_own, biases], axis=0), near)
    firsts[far] = swap(firsts[0], "tensor", far)
    out_up = jnp.concatenate([out_weight, up_weight], axis=0)

    def pieces(value):
        return [value[s * length : (s + 1) * length] for s in range(local_seqs)]

    def join(values):
        return values[0] if len(values) == 1 else jnp.concatenate(values, axis=0)

    qkv, logsums, contexts, biases = {}, {}, {}, {}
    for r in order:
        biases[r] = firsts[r][proj_rows:].reshape(1, -1)
        flat = biases[r][0]
        bias = jnp.concatenate([flat[:share], jnp.zeros((share,), BF16), flat[share : 2 * share]])
        qkv[r] = (mm(rows, firsts[r][:proj_rows], NT) + bias.astype(F32)).astype(BF16)
        got = [
            attend(part, label_columns[s], label_rows[s]) for s, part in enumerate(pieces(qkv[r]))
        ]
        contexts[r] = join([g[0] for g in got])
        logsums[r] = [g[1] for g in got]
        if r == 0:
            held = [t for t in firsts if t]
            contexts[0], out_up, down_weight, *got = hold(
                contexts[0], out_up, down_weight, *[firsts[t] for t in held]
            )
            firsts.update(zip(held, got))
            firsts.update(spread(firsts[far], near, far))
            seconds = spread(out_up, near)
            downs = spread(down_weight, near)
            seconds[far] = swap(out_up, "tensor", far)
            downs[far] = swap(down_weight, "tensor", far)
        elif r == size - 2:
            contexts[r], firsts[r + 1], seconds[far] = hold(
                contexts[r], firsts[r + 1], seconds[far]
            )
            seconds.update(spread(seconds[far], near, far))
        elif r + 1 < size:
            contexts[r], firsts[r + 1] = hold(contexts[r], firsts[r + 1])
    outs = {r: seconds[r][:share] for r in order}
    ups = {r: seconds[r][share:] for r in order}
    proj = {r: firsts[r][:proj_rows] for r in order}
    context = jnp.concatenate([contexts[r] for r in order], axis=1)
    out_all = jnp.concatenate([outs[r] for r in order], axis=0)
    attention = mm(context, out_all) + out_bias
    normal_one, rate_one = center(wide + attention)
    hidden = normal_one * first_gain + first_shift
    hidden_low = hidden.astype(BF16)
    active, slope = {}, {}
    feed = down_bias
    for r in order:
        up = mm(hidden_low, ups[r]) + biases[r][0, 2 * share : 2 * share + hidden_share].astype(F32)
        phi = 0.5 * (1.0 + lax.erf(up * 0.7071067811865476))
        active[r] = (up * phi).astype(BF16)
        slope[r] = (phi + up * jnp.exp(-0.5 * up * up) * 0.3989422804014327).astype(BF16)
        feed = feed + mm(active[r], downs[r])
        if r == far - 1:
            feed, hidden_low, downs[far] = hold(feed, hidden_low, downs[far])
            downs.update(spread(downs[far], near, far))
    normal_two, rate_two = center(hidden + feed)
    output = normal_two * second_gain + second_shift
    grad_output = cotangent.reshape(-1, width).astype(F32) * valid
    grad_two = center_back(grad_output * second_gain, normal_two, rate_two)
    grad_two_low = grad_two.astype(BF16)
    upper = [r for r in order if r & far]
    lower = [r for r in order if not r & far]

    def near_fold(group):
        group = dict(group)
        for bit in near:
            sent = [r for r in group if r & bit]
            got = swap(jnp.concatenate([group[r] for r in sent], axis=0), "tensor", bit)
            n = group[sent[0]].shape[0]
            for i, r in enumerate(sent):
                group[r ^ bit] = add_low(group[r ^ bit], got[i * n : (i + 1) * n])
            group = {r: group[r] for r in group if not r & bit}
        return [group[r] for r in sorted(group)]

    def far_fold(mine, theirs):
        return add_low(mine, swap(theirs, "tensor", far))

    def up_of(r, grad_hidden):
        up_grad = (mm(grad_two_low, downs[r], NT) * slope[r].astype(F32)).astype(BF16)
        grad_up[r] = mm(hidden_low, up_grad, TN).astype(BF16)
        up_sums[r] = jnp.sum(up_grad.astype(F32), axis=0, keepdims=True)
        return grad_hidden + mm(up_grad, ups[r], NT)

    def both_fold(group):
        group = dict(group)
        for bit in near:
            sent = [r for r in group if r & bit]
            got = swap(jnp.concatenate([group[r] for r in sent], axis=0), "tensor", bit)
            n = group[sent[0]].shape[0]
            for i, r in enumerate(sent):
                group[r ^ bit] = add_low(group[r ^ bit], got[i * n : (i + 1) * n])
            group = {r: group[r] for r in group if not r & bit}
        return group[0], group[far]

    dp_bits = bits_of(lax.axis_size("dp"))
    up_sums, grad_up = {}, {}
    grad_hidden = grad_two
    grad_down = {r: mm(active[r], grad_two_low, TN).astype(BF16) for r in order}
    grad_two_low, *held = hold(grad_two_low, *[grad_down[r] for r in order])
    grad_down = dict(zip(order, held))
    down_near, down_far = both_fold(grad_down)
    for r in upper:
        grad_hidden = up_of(r, grad_hidden)
    grad_two_low, grad_hidden, down_near, down_far, *held = hold(
        grad_two_low, grad_hidden, down_near, down_far, *[grad_up[r] for r in upper]
    )
    (up_far,) = near_fold(dict(zip(upper, held)))
    for r in lower:
        grad_hidden = up_of(r, grad_hidden)
    down_total = far_fold(down_near, down_far)
    grad_hidden, up_far, *held = hold(grad_hidden, up_far, *[grad_up[r] for r in lower])
    (up_near,) = near_fold(dict(zip(lower, held)))
    up_total = far_fold(up_near, up_far)

    grad_one = center_back(grad_hidden * first_gain, normal_one, rate_one)
    grad_one_low = grad_one.astype(BF16)
    small = jnp.concatenate(
        [
            jnp.stack(
                [
                    jnp.sum(grad_one, axis=0),
                    jnp.sum(grad_hidden * normal_one, axis=0),
                    jnp.sum(grad_hidden, axis=0),
                    jnp.sum(grad_two, axis=0),
                    jnp.sum(grad_output * normal_two, axis=0),
                    jnp.sum(grad_output, axis=0),
                    jnp.sum(output * output * valid, axis=0),
                    jnp.sum(attention * attention * valid, axis=0),
                    jnp.sum(feed * feed * valid, axis=0),
                    jnp.broadcast_to(jnp.sum(valid) / width, (width,)),
                ]
            ),
            place(up_sums, size).reshape(-1, width),
        ],
        axis=0,
    )
    small_chain = Total(small, ("tensor", "dp"))
    grad_out_all = mm(context, grad_one_low, TN).astype(BF16)
    walk = upper[::-1] + lower[::-1]
    grad_context = mm(grad_one_low, outs[walk[0]], NT).astype(BF16)
    ffn_total = jnp.concatenate([down_total, up_total], axis=0)
    grad_context, grad_one_low, grad_out_all, ffn_total = hold(
        grad_context, grad_one_low, grad_out_all, ffn_total
    )
    total_ffn = lax.psum(ffn_total, "dp")
    grad_out = {r: grad_out_all[r * share : (r + 1) * share] for r in order}
    grad_proj, stacks = {}, {}
    chains = [small_chain]
    proj_far = None

    def held_with(*values):
        got = hold(*values, *[chain.value for chain in chains])
        for chain, value in zip(chains, got[len(values) :]):
            chain.value = value
        return got[: len(values)]

    for count, r in enumerate(walk):
        for chain in chains:
            chain.step()
        if count == len(upper):
            (proj_far,) = near_fold({t: grad_proj[t] for t in upper})
        got = [
            attend_back(part, label_columns[s], label_rows[s], logsums[r][s], grad)
            for s, (part, grad) in enumerate(zip(pieces(qkv[r]), pieces(grad_context)))
        ]
        stacked = join(got)
        stacked, grad_one_low = held_with(stacked, grad_one_low)
        if count == len(upper):
            stacked, proj_far = hold(stacked, proj_far)
        for chain in chains:
            chain.step()
        stacks[r] = stacked
        sums = jnp.sum(stacked.astype(F32), axis=0)
        sums = jnp.concatenate([sums[:share], sums[2 * share :]])
        high = sums.astype(BF16)
        line = jnp.concatenate([high, (sums - high.astype(F32)).astype(BF16)])
        lines = -(-line.shape[0] // width)
        line = jnp.pad(line, (0, 16 * lines * width - line.shape[0])).reshape(16 * lines, width)
        grad_proj[r] = jnp.concatenate(
            [mm(stacked, rows, TN).astype(BF16), grad_out[r], line], axis=0
        )
        if count + 1 < size:
            grad_context = mm(grad_one_low, outs[walk[count + 1]], NT).astype(BF16)
            grad_context, grad_proj[r] = held_with(grad_context, grad_proj[r])
    (proj_near,) = near_fold({t: grad_proj[t] for t in lower})
    proj_total = far_fold(proj_near, proj_far)
    total_rows = proj_total.shape[0]
    parts = 2 if total_rows % (2 * lax.axis_size("dp")) == 0 else 1
    cut = total_rows // parts
    halves = [
        Copies(proj_total[n * cut : (n + 1) * cut], dp_bits[n:] + dp_bits[:n])
        for n in range(parts)
    ]
    for chain in halves:
        chain.step()
    fresh, *got = hold(stacks[walk[-1]], *[chain.value for chain in halves])
    stacks[walk[-1]] = fresh
    for chain, value in zip(halves, got):
        chain.value = value
    total_proj = join([chain.finish() for chain in halves])
    total_down, total_up = total_ffn[:hidden_share], total_ffn[hidden_share:]
    total_out = total_proj[proj_rows : proj_rows + share]
    grad_input = grad_one
    for r in walk:
        grad_input = grad_input + mm(stacks[r], proj[r])
    line = total_proj[proj_rows + share :].astype(F32).reshape(-1)
    total_bias = (line[: 2 * share] + line[2 * share : 4 * share]).reshape(2, share)
    total_proj = total_proj[:proj_rows].astype(F32).reshape(3, share, width).transpose(0, 2, 1)
    small = small_chain.finish()
    stats = jnp.sum(small[6:10], axis=1)
    root_means = jnp.sqrt(stats[:3] / (stats[3] * width))
    me = lax.axis_index("tensor")
    total_up_bias = lax.dynamic_slice_in_dim(small[10:].reshape(size, hidden_share), me, 1, 0)
    return (
        output.astype(BF16).reshape(tokens.shape),
        grad_input.astype(BF16).reshape(tokens.shape),
        total_proj,
        total_bias,
        total_out.astype(F32),
        small[0],
        small[1],
        small[2],
        total_up.astype(F32),
        total_up_bias.reshape(hidden_share),
        total_down.astype(F32),
        small[3],
        small[4],
        small[5],
        root_means,
    )


def solution(mesh):
    both = P(("dp", "tensor"), None, None)
    column = P(None, "tensor")
    in_specs = (
        both, P(("dp", "tensor"), None), P(None, None, "tensor"), column, P("tensor", None),
        P(), P(), P(), column, P("tensor"), P("tensor", None), P(), P(), P(), both,
    )
    out_specs = (
        both, both, P(None, None, "tensor"), column, P("tensor", None), P(), P(), P(),
        column, P("tensor"), P("tensor", None), P(), P(), P(), P(),
    )
    return jax.shard_map(shards, mesh=mesh, in_specs=in_specs, out_specs=out_specs, check_vma=False)
```

```python
import jax
import jax.numpy as jnp
from jax import lax
from jax.experimental import pallas as pl
from jax.experimental.pallas import tpu as pltpu
from jax.sharding import PartitionSpec as P


HEAD = 64
EPSILON = 1e-06
BLOCK = 512
F32 = jnp.float32
BF16 = jnp.bfloat16


NT = (((1,), (1,)), ((), ()))
NN = (((1,), (0,)), ((), ()))
TN = (((0,), (0,)), ((), ()))


def mm(left, right, dims=NN):
    return lax.dot_general(left, right, dims, preferred_element_type=F32)


def bits_of(size):
    return [1 << b for b in range(size.bit_length() - 1)]


def swap(value, axis, bit):
    size = lax.axis_size(axis)
    return lax.ppermute(value, axis, [(i, i ^ bit) for i in range(size)])


def spread(own, bits, base=0):
    pieces = {base: own}
    for bit in reversed(bits):
        for r in list(pieces):
            pieces[r | bit] = swap(pieces[r], "tensor", bit)
    return pieces


def add_low(left, right):
    return (left.astype(F32) + right.astype(F32)).astype(left.dtype)


def hold(*values):
    return lax.optimization_barrier(values)


class Copies:
    def __init__(self, value, bits):
        self.value = value
        self.todo, halved, count = [], [], value.shape[0]
        for bit in bits:
            if count % 2 or bit == bits[-1]:
                self.todo.append(("whole", bit))
            else:
                self.todo.append(("halve", bit))
                halved.append(bit)
                count //= 2
        self.todo += [("join", bit) for bit in reversed(halved)]

    def step(self):
        if not self.todo:
            return
        kind, bit = self.todo.pop(0)
        high = (lax.axis_index("dp") & bit) != 0
        value = self.value
        if kind == "halve":
            half = value.shape[0] // 2
            low_part, high_part = value[:half], value[half:]
            sent = jnp.where(high, low_part, high_part)
            kept = jnp.where(high, high_part, low_part)
            self.value = add_low(kept, swap(sent, "dp", bit))
        elif kind == "whole":
            self.value = add_low(value, swap(value, "dp", bit))
        else:
            other = swap(value, "dp", bit)
            self.value = jnp.concatenate(
                [jnp.where(high, other, value), jnp.where(high, value, other)], axis=0
            )

    def finish(self):
        while self.todo:
            self.step()
        return self.value


class Total:
    def __init__(self, value, axes):
        self.value = value
        self.todo = [(axis, bit) for axis in axes for bit in bits_of(lax.axis_size(axis))]

    def step(self):
        if self.todo:
            axis, bit = self.todo.pop(0)
            self.value = self.value + swap(self.value, axis, bit)

    def finish(self):
        while self.todo:
            self.step()
        return self.value


def place(pieces, size):
    me = lax.axis_index("tensor")
    rows = [pieces[r] for r in range(size)]
    return jnp.concatenate(
        [sum(jnp.where(me ^ r == t, rows[r], 0.0) for r in range(size)) for t in range(size)],
        axis=0,
    )


def attend_kernel(qkv_ref, all_ref, column_ref, row_ref, context_ref, logsum_ref, bias_ref):
    share = context_ref.shape[1]
    heads = share // HEAD
    scale = HEAD ** (-0.5)
    bias_ref[...] = jnp.where(column_ref[:, :1] == row_ref[...], 0.0, -1e30)
    for h in range(heads):
        at = h * HEAD
        queries = qkv_ref[:, at : at + HEAD] * jnp.asarray(scale, BF16)
        keys = all_ref[:, share + at : share + at + HEAD]
        values = all_ref[:, 2 * share + at : 2 * share + at + HEAD]
        scores = mm(keys, queries, NT) + bias_ref[...]
        maximum = jnp.max(scores, axis=0, keepdims=True)
        exponents = jnp.exp(scores - maximum)
        total = jnp.sum(exponents, axis=0, keepdims=True)
        context = mm(values.T, exponents.astype(BF16)) / total
        context_ref[:, at : at + HEAD] = context.T.astype(BF16)
        logsum_ref[h : h + 1, :] = maximum + jnp.log(total)


def attend(qkv, column, row):
    length, width = qkv.shape
    share = width // 3
    heads = share // HEAD
    block = min(BLOCK, length)
    steps = length // block
    return pl.pallas_call(
        attend_kernel,
        grid=(steps,),
        in_specs=[
            pl.BlockSpec((block, width), lambda i: (i, 0)),
            pl.BlockSpec((length, width), lambda i: (0, 0)),
            pl.BlockSpec((length, 128), lambda i: (0, 0)),
            pl.BlockSpec((1, block), lambda i: (0, i)),
        ],
        out_specs=[
            pl.BlockSpec((block, share), lambda i: (i, 0)),
            pl.BlockSpec((heads, block), lambda i: (0, i)),
        ],
        out_shape=[
            jax.ShapeDtypeStruct((length, share), BF16),
            jax.ShapeDtypeStruct((heads, length), F32),
        ],
        scratch_shapes=[pltpu.VMEM((length, block), F32)],
        cost_estimate=pl.CostEstimate(
            flops=16 * heads * length * length * HEAD,
            transcendentals=heads * length * length,
            bytes_accessed=4 * length * width,
        ),
        name="attend",
    )(qkv, qkv, column, row)


def back_kernel(
    qkv_ref, all_ref, column_ref, row_ref, logsum_ref, grad_ref, query_ref, key_ref, value_ref,
    bias_ref, key_sum, value_sum,
):
    share = grad_ref.shape[1]
    heads = share // HEAD
    scale = HEAD ** (-0.5)
    step = pl.program_id(0)
    bias_ref[...] = jnp.where(column_ref[:, :1] == row_ref[...], 0.0, -1e30)

    @pl.when(step == 0)
    def _():
        key_sum[...] = jnp.zeros_like(key_sum)
        value_sum[...] = jnp.zeros_like(value_sum)

    for h in range(heads):
        at = h * HEAD
        queries = qkv_ref[:, at : at + HEAD] * jnp.asarray(scale, BF16)
        keys = all_ref[:, share + at : share + at + HEAD]
        values = all_ref[:, 2 * share + at : 2 * share + at + HEAD]
        grad = grad_ref[:, at : at + HEAD]
        scores = mm(keys, queries, NT) + bias_ref[...]
        weights = jnp.exp(scores - logsum_ref[h : h + 1, :])
        grad_weights = mm(values, grad, NT)
        correction = jnp.sum(grad_weights * weights, axis=0, keepdims=True)
        grad_scores = (weights * (grad_weights - correction)).astype(BF16)
        value_sum[h] += mm(weights.astype(BF16), grad)
        key_sum[h] += mm(grad_scores, queries)
        grad_queries = mm(keys.T, grad_scores) * scale
        query_ref[:, at : at + HEAD] = grad_queries.T.astype(BF16)

    @pl.when(step == pl.num_programs(0) - 1)
    def _():
        for h in range(heads):
            at = h * HEAD
            key_ref[:, at : at + HEAD] = key_sum[h].astype(BF16)
            value_ref[:, at : at + HEAD] = value_sum[h].astype(BF16)


def attend_back(qkv, column, row, logsum, grad):
    length, width = qkv.shape
    share = width // 3
    heads = share // HEAD
    block = min(BLOCK, length)
    steps = length // block
    parts = pl.pallas_call(
        back_kernel,
        grid=(steps,),
        in_specs=[
            pl.BlockSpec((block, width), lambda i: (i, 0)),
            pl.BlockSpec((length, width), lambda i: (0, 0)),
            pl.BlockSpec((length, 128), lambda i: (0, 0)),
            pl.BlockSpec((1, block), lambda i: (0, i)),
            pl.BlockSpec((heads, block), lambda i: (0, i)),
            pl.BlockSpec((block, share), lambda i: (i, 0)),
        ],
        out_specs=[
            pl.BlockSpec((block, share), lambda i: (i, 0)),
            pl.BlockSpec((length, share), lambda i: (0, 0)),
            pl.BlockSpec((length, share), lambda i: (0, 0)),
        ],
        out_shape=[jax.ShapeDtypeStruct((length, share), BF16)] * 3,
        scratch_shapes=[
            pltpu.VMEM((length, block), F32),
            pltpu.VMEM((heads, length, HEAD), F32),
            pltpu.VMEM((heads, length, HEAD), F32),
        ],
        cost_estimate=pl.CostEstimate(
            flops=40 * heads * length * length * HEAD,
            transcendentals=heads * length * length,
            bytes_accessed=8 * length * width,
        ),
        name="attend_back",
    )(qkv, qkv, column, row, logsum, grad)
    return jnp.concatenate(parts, axis=1)


def center(values):
    mean = jnp.mean(values, axis=-1, keepdims=True)
    centred = values - mean
    variance = jnp.mean(centred * centred, axis=-1, keepdims=True)
    rate = lax.rsqrt(variance + EPSILON)
    return centred * rate, rate


def center_back(grad, normal, rate):
    return (
        grad
        - jnp.mean(grad, axis=-1, keepdims=True)
        - normal * jnp.mean(grad * normal, axis=-1, keepdims=True)
    ) * rate


def shards(
    tokens, segments, projections, query_value_bias, out_weight, out_bias, first_gain,
    first_shift, up_weight, up_bias, down_weight, down_bias, second_gain, second_shift, cotangent,
):
    size = lax.axis_size("tensor")
    local_seqs, length, width = tokens.shape
    share = projections.shape[2]
    hidden_share = up_weight.shape[1]
    order = range(size)
    rows = tokens.reshape(-1, width)
    wide = rows.astype(F32)
    valid = (segments != 0).astype(F32).reshape(-1, 1)
    label_rows = [segments[s : s + 1] for s in range(local_seqs)]
    label_columns = [
        jnp.broadcast_to(segments[s][:, None], (length, 128)) for s in range(local_seqs)
    ]

    proj_rows = 3 * share
    bias_rows = -(-(2 * share + hidden_share) // width)
    pad_rows = -(-bias_rows // 16) * 16
    biases = jnp.concatenate([query_value_bias.reshape(-1), up_bias])
    biases = jnp.pad(biases, (0, pad_rows * width - biases.shape[0])).reshape(pad_rows, width)
    proj_own = projections.transpose(0, 2, 1).reshape(proj_rows, width)
    bits = bits_of(size)
    near, far = bits[:-1], bits[-1]
    firsts = spread(jnp.concatenate([proj_own, biases], axis=0), near)
    firsts[far] = swap(firsts[0], "tensor", far)
    out_up = jnp.concatenate([out_weight, up_weight], axis=0)

    def pieces(value):
        return [value[s * length : (s + 1) * length] for s in range(local_seqs)]

    def join(values):
        return values[0] if len(values) == 1 else jnp.concatenate(values, axis=0)

    qkv, logsums, contexts, biases = {}, {}, {}, {}
    for r in order:
        biases[r] = firsts[r][proj_rows:].reshape(1, -1)
        flat = biases[r][0]
        bias = jnp.concatenate([flat[:share], jnp.zeros((share,), BF16), flat[share : 2 * share]])
        qkv[r] = (mm(rows, firsts[r][:proj_rows], NT) + bias.astype(F32)).astype(BF16)
        got = [
            attend(part, label_columns[s], label_rows[s]) for s, part in enumerate(pieces(qkv[r]))
        ]
        contexts[r] = join([g[0] for g in got])
        logsums[r] = [g[1] for g in got]
        if r == 0:
            held = [t for t in firsts if t]
            contexts[0], out_up, down_weight, *got = hold(
                contexts[0], out_up, down_weight, *[firsts[t] for t in held]
            )
            firsts.update(zip(held, got))
            firsts.update(spread(firsts[far], near, far))
            seconds = spread(out_up, near)
            downs = spread(down_weight, near)
            seconds[far] = swap(out_up, "tensor", far)
            downs[far] = swap(down_weight, "tensor", far)
        elif r == size - 2:
            contexts[r], firsts[r + 1], seconds[far] = hold(
                contexts[r], firsts[r + 1], seconds[far]
            )
            seconds.update(spread(seconds[far], near, far))
        elif r + 1 < size:
            contexts[r], firsts[r + 1] = hold(contexts[r], firsts[r + 1])
    outs = {r: seconds[r][:share] for r in order}
    ups = {r: seconds[r][share:] for r in order}
    proj = {r: firsts[r][:proj_rows] for r in order}
    context = jnp.concatenate([contexts[r] for r in order], axis=1)
    out_all = jnp.concatenate([outs[r] for r in order], axis=0)
    attention = mm(context, out_all) + out_bias
    normal_one, rate_one = center(wide + attention)
    hidden = normal_one * first_gain + first_shift
    hidden_low = hidden.astype(BF16)
    active, slope = {}, {}
    feed = down_bias
    for r in order:
        up = mm(hidden_low, ups[r]) + biases[r][0, 2 * share : 2 * share + hidden_share].astype(F32)
        phi = 0.5 * (1.0 + lax.erf(up * 0.7071067811865476))
        active[r] = (up * phi).astype(BF16)
        slope[r] = (phi + up * jnp.exp(-0.5 * up * up) * 0.3989422804014327).astype(BF16)
        feed = feed + mm(active[r], downs[r])
        if r == far - 1:
            feed, hidden_low, downs[far] = hold(feed, hidden_low, downs[far])
            downs.update(spread(downs[far], near, far))
    normal_two, rate_two = center(hidden + feed)
    output = normal_two * second_gain + second_shift
    grad_output = cotangent.reshape(-1, width).astype(F32) * valid
    grad_two = center_back(grad_output * second_gain, normal_two, rate_two)
    grad_two_low = grad_two.astype(BF16)
    upper = [r for r in order if r & far]
    lower = [r for r in order if not r & far]

    def near_fold(group):
        group = dict(group)
        for bit in near:
            sent = [r for r in group if r & bit]
            got = swap(jnp.concatenate([group[r] for r in sent], axis=0), "tensor", bit)
            n = group[sent[0]].shape[0]
            for i, r in enumerate(sent):
                group[r ^ bit] = add_low(group[r ^ bit], got[i * n : (i + 1) * n])
            group = {r: group[r] for r in group if not r & bit}
        return [group[r] for r in sorted(group)]

    def far_fold(mine, theirs):
        return add_low(mine, swap(theirs, "tensor", far))

    def up_of(r, grad_hidden):
        up_grad = (mm(grad_two_low, downs[r], NT) * slope[r].astype(F32)).astype(BF16)
        grad_up[r] = mm(hidden_low, up_grad, TN).astype(BF16)
        up_sums[r] = jnp.sum(up_grad.astype(F32), axis=0, keepdims=True)
        return grad_hidden + mm(up_grad, ups[r], NT)

    def both_fold(group):
        group = dict(group)
        for bit in near:
            sent = [r for r in group if r & bit]
            got = swap(jnp.concatenate([group[r] for r in sent], axis=0), "tensor", bit)
            n = group[sent[0]].shape[0]
            for i, r in enumerate(sent):
                group[r ^ bit] = add_low(group[r ^ bit], got[i * n : (i + 1) * n])
            group = {r: group[r] for r in group if not r & bit}
        return group[0], group[far]

    dp_bits = bits_of(lax.axis_size("dp"))
    up_sums, grad_up = {}, {}
    grad_hidden = grad_two
    grad_down = {r: mm(active[r], grad_two_low, TN).astype(BF16) for r in order}
    grad_two_low, *held = hold(grad_two_low, *[grad_down[r] for r in order])
    grad_down = dict(zip(order, held))
    down_near, down_far = both_fold(grad_down)
    for r in upper:
        grad_hidden = up_of(r, grad_hidden)
    grad_two_low, grad_hidden, down_near, down_far, *held = hold(
        grad_two_low, grad_hidden, down_near, down_far, *[grad_up[r] for r in upper]
    )
    (up_far,) = near_fold(dict(zip(upper, held)))
    for r in lower:
        grad_hidden = up_of(r, grad_hidden)
    down_total = far_fold(down_near, down_far)
    grad_hidden, up_far, *held = hold(grad_hidden, up_far, *[grad_up[r] for r in lower])
    (up_near,) = near_fold(dict(zip(lower, held)))
    up_total = far_fold(up_near, up_far)

    grad_one = center_back(grad_hidden * first_gain, normal_one, rate_one)
    grad_one_low = grad_one.astype(BF16)
    small = jnp.concatenate(
        [
            jnp.stack(
                [
                    jnp.sum(grad_one, axis=0),
                    jnp.sum(grad_hidden * normal_one, axis=0),
                    jnp.sum(grad_hidden, axis=0),
                    jnp.sum(grad_two, axis=0),
                    jnp.sum(grad_output * normal_two, axis=0),
                    jnp.sum(grad_output, axis=0),
                    jnp.sum(output * output * valid, axis=0),
                    jnp.sum(attention * attention * valid, axis=0),
                    jnp.sum(feed * feed * valid, axis=0),
                    jnp.broadcast_to(jnp.sum(valid) / width, (width,)),
                ]
            ),
            place(up_sums, size).reshape(-1, width),
        ],
        axis=0,
    )
    small_chain = Total(small, ("tensor", "dp"))
    grad_out_all = mm(context, grad_one_low, TN).astype(BF16)
    walk = upper[::-1] + lower[::-1]
    grad_context = mm(grad_one_low, outs[walk[0]], NT).astype(BF16)
    grad_context, grad_one_low, grad_out_all, down_total = hold(
        grad_context, grad_one_low, grad_out_all, down_total
    )
    total_ffn = None
    grad_out = {r: grad_out_all[r * share : (r + 1) * share] for r in order}
    grad_proj, stacks = {}, {}
    chains = [small_chain]
    proj_far = None

    def held_with(*values):
        got = hold(*values, *[chain.value for chain in chains])
        for chain, value in zip(chains, got[len(values) :]):
            chain.value = value
        return got[: len(values)]

    for count, r in enumerate(walk):
        for chain in chains:
            chain.step()
        if count == len(upper):
            (proj_far,) = near_fold({t: grad_proj[t] for t in upper})
        got = [
            attend_back(part, label_columns[s], label_rows[s], logsums[r][s], grad)
            for s, (part, grad) in enumerate(zip(pieces(qkv[r]), pieces(grad_context)))
        ]
        stacked = join(got)
        if count == 0:
            ffn_total = jnp.concatenate([down_total, up_total], axis=0)
            stacked, grad_one_low, ffn_total = held_with(stacked, grad_one_low, ffn_total)
            total_ffn = lax.psum(ffn_total, "dp")
        else:
            stacked, grad_one_low = held_with(stacked, grad_one_low)
        if count == len(upper):
            stacked, proj_far = hold(stacked, proj_far)
        for chain in chains:
            chain.step()
        stacks[r] = stacked
        sums = jnp.sum(stacked.astype(F32), axis=0)
        sums = jnp.concatenate([sums[:share], sums[2 * share :]])
        high = sums.astype(BF16)
        line = jnp.concatenate([high, (sums - high.astype(F32)).astype(BF16)])
        lines = -(-line.shape[0] // width)
        line = jnp.pad(line, (0, 16 * lines * width - line.shape[0])).reshape(16 * lines, width)
        grad_proj[r] = jnp.concatenate(
            [mm(stacked, rows, TN).astype(BF16), grad_out[r], line], axis=0
        )
        if count + 1 < size:
            grad_context = mm(grad_one_low, outs[walk[count + 1]], NT).astype(BF16)
            grad_context, grad_proj[r] = held_with(grad_context, grad_proj[r])
    (proj_near,) = near_fold({t: grad_proj[t] for t in lower})
    proj_total = far_fold(proj_near, proj_far)
    total_rows = proj_total.shape[0]
    parts = 2 if total_rows % (2 * lax.axis_size("dp")) == 0 else 1
    cut = total_rows // parts
    halves = [
        Copies(proj_total[n * cut : (n + 1) * cut], dp_bits[n:] + dp_bits[:n])
        for n in range(parts)
    ]
    for chain in halves:
        chain.step()
    fresh, *got = hold(stacks[walk[-1]], *[chain.value for chain in halves])
    stacks[walk[-1]] = fresh
    for chain, value in zip(halves, got):
        chain.value = value
    for chain in halves:
        chain.step()
        chain.step()
    total_ffn, *got = hold(total_ffn, *[chain.value for chain in halves])
    for chain, value in zip(halves, got):
        chain.value = value
    total_proj = join([chain.finish() for chain in halves])
    total_down, total_up = total_ffn[:hidden_share], total_ffn[hidden_share:]
    total_out = total_proj[proj_rows : proj_rows + share]
    grad_input = grad_one
    for r in walk:
        grad_input = grad_input + mm(stacks[r], proj[r])
    line = total_proj[proj_rows + share :].astype(F32).reshape(-1)
    total_bias = (line[: 2 * share] + line[2 * share : 4 * share]).reshape(2, share)
    total_proj = total_proj[:proj_rows].astype(F32).reshape(3, share, width).transpose(0, 2, 1)
    small = small_chain.finish()
    stats = jnp.sum(small[6:10], axis=1)
    root_means = jnp.sqrt(stats[:3] / (stats[3] * width))
    me = lax.axis_index("tensor")
    total_up_bias = lax.dynamic_slice_in_dim(small[10:].reshape(size, hidden_share), me, 1, 0)
    return (
        output.astype(BF16).reshape(tokens.shape),
        grad_input.astype(BF16).reshape(tokens.shape),
        total_proj,
        total_bias,
        total_out.astype(F32),
        small[0],
        small[1],
        small[2],
        total_up.astype(F32),
        total_up_bias.reshape(hidden_share),
        total_down.astype(F32),
        small[3],
        small[4],
        small[5],
        root_means,
    )


def solution(mesh):
    both = P(("dp", "tensor"), None, None)
    column = P(None, "tensor")
    in_specs = (
        both, P(("dp", "tensor"), None), P(None, None, "tensor"), column, P("tensor", None),
        P(), P(), P(), column, P("tensor"), P("tensor", None), P(), P(), P(), both,
    )
    out_specs = (
        both, both, P(None, None, "tensor"), column, P("tensor", None), P(), P(), P(),
        column, P("tensor"), P("tensor", None), P(), P(), P(), P(),
    )
    return jax.shard_map(shards, mesh=mesh, in_specs=in_specs, out_specs=out_specs, check_vma=False)
```

```python
import jax
import jax.numpy as jnp
from jax import lax
from jax.experimental import pallas as pl
from jax.experimental.pallas import tpu as pltpu
from jax.sharding import PartitionSpec as P


HEAD = 64
EPSILON = 1e-06
BLOCK = 512
F32 = jnp.float32
BF16 = jnp.bfloat16


NT = (((1,), (1,)), ((), ()))
NN = (((1,), (0,)), ((), ()))
TN = (((0,), (0,)), ((), ()))


def mm(left, right, dims=NN):
    return lax.dot_general(left, right, dims, preferred_element_type=F32)


def bits_of(size):
    return [1 << b for b in range(size.bit_length() - 1)]


def swap(value, axis, bit):
    size = lax.axis_size(axis)
    return lax.ppermute(value, axis, [(i, i ^ bit) for i in range(size)])


def spread(own, bits, base=0):
    pieces = {base: own}
    for bit in reversed(bits):
        for r in list(pieces):
            pieces[r | bit] = swap(pieces[r], "tensor", bit)
    return pieces


def add_low(left, right):
    return (left.astype(F32) + right.astype(F32)).astype(left.dtype)


def hold(*values):
    return lax.optimization_barrier(values)


class Copies:
    def __init__(self, value, bits):
        self.value = value
        self.todo, halved, count = [], [], value.shape[0]
        for bit in bits:
            if count % 2 or bit == bits[-1]:
                self.todo.append(("whole", bit))
            else:
                self.todo.append(("halve", bit))
                halved.append(bit)
                count //= 2
        self.todo += [("join", bit) for bit in reversed(halved)]

    def step(self):
        if not self.todo:
            return
        kind, bit = self.todo.pop(0)
        high = (lax.axis_index("dp") & bit) != 0
        value = self.value
        if kind == "halve":
            half = value.shape[0] // 2
            low_part, high_part = value[:half], value[half:]
            sent = jnp.where(high, low_part, high_part)
            kept = jnp.where(high, high_part, low_part)
            self.value = add_low(kept, swap(sent, "dp", bit))
        elif kind == "whole":
            self.value = add_low(value, swap(value, "dp", bit))
        else:
            other = swap(value, "dp", bit)
            self.value = jnp.concatenate(
                [jnp.where(high, other, value), jnp.where(high, value, other)], axis=0
            )

    def finish(self):
        while self.todo:
            self.step()
        return self.value


class Total:
    def __init__(self, value, axes):
        self.value = value
        self.todo = [(axis, bit) for axis in axes for bit in bits_of(lax.axis_size(axis))]

    def step(self):
        if self.todo:
            axis, bit = self.todo.pop(0)
            self.value = self.value + swap(self.value, axis, bit)

    def finish(self):
        while self.todo:
            self.step()
        return self.value


def place(pieces, size):
    me = lax.axis_index("tensor")
    rows = [pieces[r] for r in range(size)]
    return jnp.concatenate(
        [sum(jnp.where(me ^ r == t, rows[r], 0.0) for r in range(size)) for t in range(size)],
        axis=0,
    )


def attend_kernel(qkv_ref, all_ref, column_ref, row_ref, context_ref, logsum_ref, bias_ref):
    share = context_ref.shape[1]
    heads = share // HEAD
    scale = HEAD ** (-0.5)
    bias_ref[...] = jnp.where(column_ref[:, :1] == row_ref[...], 0.0, -1e30)
    for h in range(heads):
        at = h * HEAD
        queries = qkv_ref[:, at : at + HEAD] * jnp.asarray(scale, BF16)
        keys = all_ref[:, share + at : share + at + HEAD]
        values = all_ref[:, 2 * share + at : 2 * share + at + HEAD]
        scores = mm(keys, queries, NT) + bias_ref[...]
        maximum = jnp.max(scores, axis=0, keepdims=True)
        exponents = jnp.exp(scores - maximum)
        total = jnp.sum(exponents, axis=0, keepdims=True)
        context = mm(values.T, exponents.astype(BF16)) / total
        context_ref[:, at : at + HEAD] = context.T.astype(BF16)
        logsum_ref[h : h + 1, :] = maximum + jnp.log(total)


def attend(qkv, column, row):
    length, width = qkv.shape
    share = width // 3
    heads = share // HEAD
    block = min(BLOCK, length)
    steps = length // block
    return pl.pallas_call(
        attend_kernel,
        grid=(steps,),
        in_specs=[
            pl.BlockSpec((block, width), lambda i: (i, 0)),
            pl.BlockSpec((length, width), lambda i: (0, 0)),
            pl.BlockSpec((length, 128), lambda i: (0, 0)),
            pl.BlockSpec((1, block), lambda i: (0, i)),
        ],
        out_specs=[
            pl.BlockSpec((block, share), lambda i: (i, 0)),
            pl.BlockSpec((heads, block), lambda i: (0, i)),
        ],
        out_shape=[
            jax.ShapeDtypeStruct((length, share), BF16),
            jax.ShapeDtypeStruct((heads, length), F32),
        ],
        scratch_shapes=[pltpu.VMEM((length, block), F32)],
        cost_estimate=pl.CostEstimate(
            flops=16 * heads * length * length * HEAD,
            transcendentals=heads * length * length,
            bytes_accessed=4 * length * width,
        ),
        name="attend",
    )(qkv, qkv, column, row)


def back_kernel(
    qkv_ref, all_ref, column_ref, row_ref, logsum_ref, grad_ref, out_ref, bias_ref, key_sum,
    value_sum,
):
    share = grad_ref.shape[1]
    heads = share // HEAD
    scale = HEAD ** (-0.5)
    step = pl.program_id(0)
    block = grad_ref.shape[0]
    bias_ref[...] = jnp.where(column_ref[:, :1] == row_ref[...], 0.0, -1e30)

    @pl.when(step == 0)
    def _():
        key_sum[...] = jnp.zeros_like(key_sum)
        value_sum[...] = jnp.zeros_like(value_sum)

    for h in range(heads):
        at = h * HEAD
        queries = qkv_ref[:, at : at + HEAD] * jnp.asarray(scale, BF16)
        keys = all_ref[:, share + at : share + at + HEAD]
        values = all_ref[:, 2 * share + at : 2 * share + at + HEAD]
        grad = grad_ref[:, at : at + HEAD]
        scores = mm(keys, queries, NT) + bias_ref[...]
        weights = jnp.exp(scores - logsum_ref[h : h + 1, :])
        grad_weights = mm(values, grad, NT)
        correction = jnp.sum(grad_weights * weights, axis=0, keepdims=True)
        grad_scores = (weights * (grad_weights - correction)).astype(BF16)
        value_sum[h] += mm(weights.astype(BF16), grad)
        key_sum[h] += mm(grad_scores, queries)
        grad_queries = mm(keys.T, grad_scores) * scale
        here = pl.ds(pl.multiple_of(step * block, block), block)
        out_ref[here, at : at + HEAD] = grad_queries.T.astype(BF16)

    @pl.when(step == pl.num_programs(0) - 1)
    def _():
        for h in range(heads):
            at = h * HEAD
            out_ref[:, share + at : share + at + HEAD] = key_sum[h].astype(BF16)
            out_ref[:, 2 * share + at : 2 * share + at + HEAD] = value_sum[h].astype(BF16)


def attend_back(qkv, column, row, logsum, grad):
    length, width = qkv.shape
    share = width // 3
    heads = share // HEAD
    block = min(BLOCK, length)
    steps = length // block
    return pl.pallas_call(
        back_kernel,
        grid=(steps,),
        in_specs=[
            pl.BlockSpec((block, width), lambda i: (i, 0)),
            pl.BlockSpec((length, width), lambda i: (0, 0)),
            pl.BlockSpec((length, 128), lambda i: (0, 0)),
            pl.BlockSpec((1, block), lambda i: (0, i)),
            pl.BlockSpec((heads, block), lambda i: (0, i)),
            pl.BlockSpec((block, share), lambda i: (i, 0)),
        ],
        out_specs=pl.BlockSpec((length, width), lambda i: (0, 0)),
        out_shape=jax.ShapeDtypeStruct((length, width), BF16),
        scratch_shapes=[
            pltpu.VMEM((length, block), F32),
            pltpu.VMEM((heads, length, HEAD), F32),
            pltpu.VMEM((heads, length, HEAD), F32),
        ],
        cost_estimate=pl.CostEstimate(
            flops=40 * heads * length * length * HEAD,
            transcendentals=heads * length * length,
            bytes_accessed=8 * length * width,
        ),
        name="attend_back",
    )(qkv, qkv, column, row, logsum, grad)


def center(values):
    mean = jnp.mean(values, axis=-1, keepdims=True)
    centred = values - mean
    variance = jnp.mean(centred * centred, axis=-1, keepdims=True)
    rate = lax.rsqrt(variance + EPSILON)
    return centred * rate, rate


def center_back(grad, normal, rate):
    return (
        grad
        - jnp.mean(grad, axis=-1, keepdims=True)
        - normal * jnp.mean(grad * normal, axis=-1, keepdims=True)
    ) * rate


def shards(
    tokens, segments, projections, query_value_bias, out_weight, out_bias, first_gain,
    first_shift, up_weight, up_bias, down_weight, down_bias, second_gain, second_shift, cotangent,
):
    size = lax.axis_size("tensor")
    local_seqs, length, width = tokens.shape
    share = projections.shape[2]
    hidden_share = up_weight.shape[1]
    order = range(size)
    rows = tokens.reshape(-1, width)
    wide = rows.astype(F32)
    valid = (segments != 0).astype(F32).reshape(-1, 1)
    label_rows = [segments[s : s + 1] for s in range(local_seqs)]
    label_columns = [
        jnp.broadcast_to(segments[s][:, None], (length, 128)) for s in range(local_seqs)
    ]

    proj_rows = 3 * share
    bias_rows = -(-(2 * share + hidden_share) // width)
    pad_rows = -(-bias_rows // 16) * 16
    biases = jnp.concatenate([query_value_bias.reshape(-1), up_bias])
    biases = jnp.pad(biases, (0, pad_rows * width - biases.shape[0])).reshape(pad_rows, width)
    proj_own = projections.transpose(0, 2, 1).reshape(proj_rows, width)
    bits = bits_of(size)
    near, far = bits[:-1], bits[-1]
    firsts = spread(jnp.concatenate([proj_own, biases], axis=0), near)
    firsts[far] = swap(firsts[0], "tensor", far)
    out_up = jnp.concatenate([out_weight, up_weight], axis=0)

    def pieces(value):
        return [value[s * length : (s + 1) * length] for s in range(local_seqs)]

    def join(values):
        return values[0] if len(values) == 1 else jnp.concatenate(values, axis=0)

    qkv, logsums, contexts, biases = {}, {}, {}, {}
    for r in order:
        biases[r] = firsts[r][proj_rows:].reshape(1, -1)
        flat = biases[r][0]
        bias = jnp.concatenate([flat[:share], jnp.zeros((share,), BF16), flat[share : 2 * share]])
        qkv[r] = (mm(rows, firsts[r][:proj_rows], NT) + bias.astype(F32)).astype(BF16)
        got = [
            attend(part, label_columns[s], label_rows[s]) for s, part in enumerate(pieces(qkv[r]))
        ]
        contexts[r] = join([g[0] for g in got])
        logsums[r] = [g[1] for g in got]
        if r == 0:
            held = [t for t in firsts if t]
            contexts[0], out_up, down_weight, *got = hold(
                contexts[0], out_up, down_weight, *[firsts[t] for t in held]
            )
            firsts.update(zip(held, got))
            firsts.update(spread(firsts[far], near, far))
            seconds = spread(out_up, near)
            downs = spread(down_weight, near)
            seconds[far] = swap(out_up, "tensor", far)
            downs[far] = swap(down_weight, "tensor", far)
        elif r == size - 2:
            contexts[r], firsts[r + 1], seconds[far] = hold(
                contexts[r], firsts[r + 1], seconds[far]
            )
            seconds.update(spread(seconds[far], near, far))
        elif r + 1 < size:
            contexts[r], firsts[r + 1] = hold(contexts[r], firsts[r + 1])
    outs = {r: seconds[r][:share] for r in order}
    ups = {r: seconds[r][share:] for r in order}
    proj = {r: firsts[r][:proj_rows] for r in order}
    context = jnp.concatenate([contexts[r] for r in order], axis=1)
    out_all = jnp.concatenate([outs[r] for r in order], axis=0)
    attention = mm(context, out_all) + out_bias
    normal_one, rate_one = center(wide + attention)
    hidden = normal_one * first_gain + first_shift
    hidden_low = hidden.astype(BF16)
    active, slope = {}, {}
    feed = down_bias
    for r in order:
        up = mm(hidden_low, ups[r]) + biases[r][0, 2 * share : 2 * share + hidden_share].astype(F32)
        phi = 0.5 * (1.0 + lax.erf(up * 0.7071067811865476))
        active[r] = (up * phi).astype(BF16)
        slope[r] = (phi + up * jnp.exp(-0.5 * up * up) * 0.3989422804014327).astype(BF16)
        feed = feed + mm(active[r], downs[r])
        if r == far - 1:
            feed, hidden_low, downs[far] = hold(feed, hidden_low, downs[far])
            downs.update(spread(downs[far], near, far))
    normal_two, rate_two = center(hidden + feed)
    output = normal_two * second_gain + second_shift
    grad_output = cotangent.reshape(-1, width).astype(F32) * valid
    grad_two = center_back(grad_output * second_gain, normal_two, rate_two)
    grad_two_low = grad_two.astype(BF16)
    upper = [r for r in order if r & far]
    lower = [r for r in order if not r & far]

    def near_fold(group):
        group = dict(group)
        for bit in near:
            sent = [r for r in group if r & bit]
            got = swap(jnp.concatenate([group[r] for r in sent], axis=0), "tensor", bit)
            n = group[sent[0]].shape[0]
            for i, r in enumerate(sent):
                group[r ^ bit] = add_low(group[r ^ bit], got[i * n : (i + 1) * n])
            group = {r: group[r] for r in group if not r & bit}
        return [group[r] for r in sorted(group)]

    def far_fold(mine, theirs):
        return add_low(mine, swap(theirs, "tensor", far))

    def up_of(r, grad_hidden):
        up_grad = (mm(grad_two_low, downs[r], NT) * slope[r].astype(F32)).astype(BF16)
        grad_up[r] = mm(hidden_low, up_grad, TN).astype(BF16)
        up_sums[r] = jnp.sum(up_grad.astype(F32), axis=0, keepdims=True)
        return grad_hidden + mm(up_grad, ups[r], NT)

    def both_fold(group):
        group = dict(group)
        for bit in near:
            sent = [r for r in group if r & bit]
            got = swap(jnp.concatenate([group[r] for r in sent], axis=0), "tensor", bit)
            n = group[sent[0]].shape[0]
            for i, r in enumerate(sent):
                group[r ^ bit] = add_low(group[r ^ bit], got[i * n : (i + 1) * n])
            group = {r: group[r] for r in group if not r & bit}
        return group[0], group[far]

    dp_bits = bits_of(lax.axis_size("dp"))
    up_sums, grad_up = {}, {}
    grad_hidden = grad_two
    grad_down = {r: mm(active[r], grad_two_low, TN).astype(BF16) for r in order}
    grad_two_low, *held = hold(grad_two_low, *[grad_down[r] for r in order])
    grad_down = dict(zip(order, held))
    down_near, down_far = both_fold(grad_down)
    for r in upper[:1]:
        grad_hidden = up_of(r, grad_hidden)
    grad_two_low, grad_hidden, down_near, down_far = hold(
        grad_two_low, grad_hidden, down_near, down_far
    )
    for r in upper[1:]:
        grad_hidden = up_of(r, grad_hidden)
    grad_two_low, grad_hidden, *held = hold(
        grad_two_low, grad_hidden, *[grad_up[r] for r in upper]
    )
    (up_far,) = near_fold(dict(zip(upper, held)))
    for r in lower:
        grad_hidden = up_of(r, grad_hidden)
    down_total = far_fold(down_near, down_far)
    grad_hidden, up_far, *held = hold(grad_hidden, up_far, *[grad_up[r] for r in lower])
    (up_near,) = near_fold(dict(zip(lower, held)))
    up_total = far_fold(up_near, up_far)

    grad_one = center_back(grad_hidden * first_gain, normal_one, rate_one)
    grad_one_low = grad_one.astype(BF16)
    small = jnp.concatenate(
        [
            jnp.stack(
                [
                    jnp.sum(grad_one, axis=0),
                    jnp.sum(grad_hidden * normal_one, axis=0),
                    jnp.sum(grad_hidden, axis=0),
                    jnp.sum(grad_two, axis=0),
                    jnp.sum(grad_output * normal_two, axis=0),
                    jnp.sum(grad_output, axis=0),
                    jnp.sum(output * output * valid, axis=0),
                    jnp.sum(attention * attention * valid, axis=0),
                    jnp.sum(feed * feed * valid, axis=0),
                    jnp.broadcast_to(jnp.sum(valid) / width, (width,)),
                ]
            ),
            place(up_sums, size).reshape(-1, width),
        ],
        axis=0,
    )
    small_chain = Total(small, ("tensor", "dp"))
    grad_out_all = mm(context, grad_one_low, TN).astype(BF16)
    walk = upper[::-1] + lower[::-1]
    grad_context = mm(grad_one_low, outs[walk[0]], NT).astype(BF16)
    grad_out = {r: grad_out_all[r * share : (r + 1) * share] for r in order}
    out_near, out_far = both_fold(grad_out)
    grad_context, grad_one_low, out_near, out_far, down_total = hold(
        grad_context, grad_one_low, out_near, out_far, down_total
    )
    out_total = far_fold(out_near, out_far)
    total_ffn = None
    grad_proj, stacks = {}, {}
    chains = [small_chain]
    proj_far = None

    def held_with(*values):
        got = hold(*values, *[chain.value for chain in chains])
        for chain, value in zip(chains, got[len(values) :]):
            chain.value = value
        return got[: len(values)]

    for count, r in enumerate(walk):
        for chain in chains:
            chain.step()
        if count == len(upper):
            (proj_far,) = near_fold({t: grad_proj[t] for t in upper})
        got = [
            attend_back(part, label_columns[s], label_rows[s], logsums[r][s], grad)
            for s, (part, grad) in enumerate(zip(pieces(qkv[r]), pieces(grad_context)))
        ]
        stacked = join(got)
        if count == 0:
            ffn_total = jnp.concatenate([down_total, up_total, out_total], axis=0)
            stacked, grad_one_low, ffn_total = held_with(stacked, grad_one_low, ffn_total)
            total_ffn = lax.psum(ffn_total, "dp")
        else:
            stacked, grad_one_low = held_with(stacked, grad_one_low)
        if count == len(upper):
            stacked, proj_far = hold(stacked, proj_far)
        for chain in chains:
            chain.step()
        stacks[r] = stacked
        sums = jnp.sum(stacked.astype(F32), axis=0)
        sums = jnp.concatenate([sums[:share], sums[2 * share :]])
        high = sums.astype(BF16)
        line = jnp.concatenate([high, (sums - high.astype(F32)).astype(BF16)])
        lines = -(-line.shape[0] // width)
        line = jnp.pad(line, (0, 16 * lines * width - line.shape[0])).reshape(16 * lines, width)
        grad_proj[r] = jnp.concatenate(
            [mm(stacked, rows, TN).astype(BF16), line], axis=0
        )
        if count + 1 < size:
            grad_context = mm(grad_one_low, outs[walk[count + 1]], NT).astype(BF16)
            grad_context, grad_proj[r] = held_with(grad_context, grad_proj[r])
    (proj_near,) = near_fold({t: grad_proj[t] for t in lower})
    proj_total = far_fold(proj_near, proj_far)
    total_rows = proj_total.shape[0]
    parts = 2 if total_rows % (2 * lax.axis_size("dp")) == 0 else 1
    cut = total_rows // parts
    halves = [
        Copies(proj_total[n * cut : (n + 1) * cut], dp_bits[n:] + dp_bits[:n])
        for n in range(parts)
    ]
    for chain in halves:
        chain.step()
    fresh, *got = hold(stacks[walk[-1]], *[chain.value for chain in halves])
    stacks[walk[-1]] = fresh
    for chain, value in zip(halves, got):
        chain.value = value
    for chain in halves:
        chain.step()
        chain.step()
        chain.step()
    total_ffn, *got = hold(total_ffn, *[chain.value for chain in halves])
    for chain, value in zip(halves, got):
        chain.value = value
    total_proj = join([chain.finish() for chain in halves])
    total_down, total_up = total_ffn[:hidden_share], total_ffn[hidden_share:][:width]
    total_out = total_ffn[hidden_share + width :]
    grad_input = grad_one
    for r in walk:
        grad_input = grad_input + mm(stacks[r], proj[r])
    line = total_proj[proj_rows:].astype(F32).reshape(-1)
    total_bias = (line[: 2 * share] + line[2 * share : 4 * share]).reshape(2, share)
    total_proj = total_proj[:proj_rows].astype(F32).reshape(3, share, width).transpose(0, 2, 1)
    small = small_chain.finish()
    stats = jnp.sum(small[6:10], axis=1)
    root_means = jnp.sqrt(stats[:3] / (stats[3] * width))
    me = lax.axis_index("tensor")
    total_up_bias = lax.dynamic_slice_in_dim(small[10:].reshape(size, hidden_share), me, 1, 0)
    return (
        output.astype(BF16).reshape(tokens.shape),
        grad_input.astype(BF16).reshape(tokens.shape),
        total_proj,
        total_bias,
        total_out.astype(F32),
        small[0],
        small[1],
        small[2],
        total_up.astype(F32),
        total_up_bias.reshape(hidden_share),
        total_down.astype(F32),
        small[3],
        small[4],
        small[5],
        root_means,
    )


def solution(mesh):
    both = P(("dp", "tensor"), None, None)
    column = P(None, "tensor")
    in_specs = (
        both, P(("dp", "tensor"), None), P(None, None, "tensor"), column, P("tensor", None),
        P(), P(), P(), column, P("tensor"), P("tensor", None), P(), P(), P(), both,
    )
    out_specs = (
        both, both, P(None, None, "tensor"), column, P("tensor", None), P(), P(), P(),
        column, P("tensor"), P("tensor", None), P(), P(), P(), P(),
    )
    return jax.shard_map(shards, mesh=mesh, in_specs=in_specs, out_specs=out_specs, check_vma=False)
```
